256 devices in a mesh: ctx: 32 (over y, z), head: 8 (over x, core).
Axes of the slice: x: 4, y: 4, z: 8, core: 2. Of those that a mesh axis runs over, the one named last changes fastest.
Arguments:
- qkv: bfloat16 [32768, 3, 32, 128], P(('ctx', 'head')), may hold values from -50 to 50, as said below
- lengths: int32 [8], replicated, may hold values from 1 to 16384, 32768 in all
- reg: float32 [32], replicated, may hold values from 0.5 to 2
Outputs:
- mixed: bfloat16 [32768, 32, 128], P(('ctx', 'head'))
The draws below stay inside these ranges and needn't reach their ends.
Inputs may be any that keep to these rules, and one draw needn't show every extreme that they name: `qkv`: entries of queries, keys and values; each head's channels have scales that differ by up to a factor of ten or more. `lengths`: the longest document has exactly 16384 tokens.
All inputs are finite; a program needn't handle non-finite values.
Results may differ from the reference program's by a relative error of at most 0.0056.
Values may be sent and summed in bfloat16 or wider, within the bound.
No kernel may reach another device: no remote copies, remote signals or barrier semaphores. Data moves between devices by JAX's collectives and lax.ppermute only.
A program may use at most 128 MiB of HBM per device.

```python
import math
import jax
import jax.numpy as jnp
import numpy as np
from jax import lax

HEADS = 32
HD = 128
TOK_DEV = 1024
ITERS = 10
DOCS = 8
TOKENS = 32768


def draw_qkv(key, part):
    base_key, scale_key = jax.random.split(jax.random.fold_in(key, 17), 2)
    base = jax.random.truncated_normal(base_key, -5.0, 5.0, (TOKENS, 3, HEADS, HD), jnp.float32)
    spread = jnp.exp(jax.random.uniform(scale_key, (3, HEADS, HD), jnp.float32, 0.0, math.log(10.0)))
    return (base * spread[None]).astype(jnp.bfloat16)


def split_up(number_of, total, most, lean):
    loads = [(1 << 20) // math.isqrt(standing ** lean) + 1 for standing in range(2, number_of + 1)]
    surplus, holding = total - most - (number_of - 1), [1] * (number_of - 1)
    while surplus > 0:
        free = [i for i in range(number_of - 1) if holding[i] < most]
        whole, remaining = sum([loads[i] for i in free]), surplus
        for i in free:
            more = min(most - holding[i], max(1, remaining * loads[i] // whole), surplus)
            holding[i] = holding[i] + more
            surplus = surplus - more
    return np.array([most] + holding)


def ragged(key, count, total, limit, lean):
    if count == 2:
        one = jax.random.randint(key, (), max(1, total - limit), min(limit, total - 1) + 1)
        return jnp.stack([one, total - one])
    sizes = jnp.asarray(split_up(count, total, limit, lean), jnp.int32)
    pairs = (count - 1) // 2
    donor, sink = sizes[1:1 + 2 * pairs:2], sizes[2:2 + 2 * pairs:2]
    room = jnp.minimum(donor - 1, limit - sink)
    shifted = jax.random.randint(jax.random.fold_in(key, 1), (pairs,), 0, 1 << 20) % (room + 1)
    sizes = sizes.at[1:1 + 2 * pairs:2].set(donor - shifted).at[2:2 + 2 * pairs:2].set(sink + shifted)
    return sizes[jax.random.permutation(jax.random.fold_in(key, 2), count)]


def setup_inputs(seed: int = 0) -> dict:
    key_list = jax.random.split(jax.random.key(seed), 4)
    return {
        "qkv": draw_qkv(jax.random.fold_in(key_list[3], 71), 0),
        "lengths": ragged(key_list[1], DOCS, TOKENS, TOKENS // 2, 2).astype(jnp.int32),
        "reg": jnp.clip(jnp.exp(jax.random.uniform(key_list[2], (HEADS,), jnp.float32, math.log(0.5), math.log(2.0))), 0.5, 2.0),
    }


HIGHEST = lax.Precision.HIGHEST

def normalize(rows):
    rows = rows.astype(jnp.float32)
    return rows * lax.rsqrt(lax.optimization_barrier(jnp.mean(rows * rows, axis=-1, keepdims=True)) + 1e-06) / math.sqrt(rows.shape[-1])

def doc_marks(lengths, offset, row_count):
    doc_ends = jnp.cumsum(lengths).astype(jnp.int32)
    starts = (doc_ends - lengths).astype(jnp.int32)
    places = (offset + jnp.arange(row_count, dtype=jnp.int32)).astype(jnp.int32)
    start_mark = jnp.any(places[:, None] == starts[None, :], axis=1)
    segment = lax.optimization_barrier(jnp.sum((starts[None, :] <= places[:, None]).astype(jnp.int32), axis=1))
    return (starts, start_mark, segment)

def block_sums(key_rows, value_rows, segment, start_mark):
    in_tail = (segment == segment[:, -1:]).astype(jnp.float32)
    reset_flag = lax.optimization_barrier(jnp.max(start_mark.astype(jnp.float32), axis=1))
    key_full = key_rows.astype(jnp.float32)
    weighted = key_full * in_tail[:, :, None, None]
    key_sum = jnp.einsum('cbhd,cbhe->chde', weighted, key_full, precision=HIGHEST)
    value_sum = jnp.einsum('cbhd,cbhe->chde', value_rows.astype(jnp.float32) * in_tail[:, :, None, None], key_full, precision=HIGHEST)
    return (reset_flag, key_sum, value_sum)

def solve_blocks(queries, key_rows, value_rows, segment, start_mark, key_entry, value_entry, damping):
    block_len = queries.shape[1]
    valid = (jnp.cumsum(start_mark.astype(jnp.int32), axis=1) == 0).astype(jnp.float32)[:, :, None, None]
    lower = jnp.arange(block_len)[:, None] >= jnp.arange(block_len)[None, :]
    same = ((segment[:, :, None] == segment[:, None, :]) & lower[None]).astype(jnp.float32)[:, None]

    def block_scores(vectors):
        scores = jnp.einsum('cbhd,cihd->chbi', vectors.astype(jnp.bfloat16), key_rows, preferred_element_type=jnp.float32) * same
        return scores.astype(jnp.bfloat16)

    def operate(direction):
        from_state = jnp.einsum('chde,cbhe->cbhd', key_entry, direction, precision=HIGHEST) * valid
        in_block = jnp.einsum('chbi,cihd->cbhd', block_scores(direction), key_rows, preferred_element_type=jnp.float32)
        return from_state + in_block + damping[None, None, :, None] * direction
    solution = jnp.zeros_like(queries)
    residual = queries
    direction = queries
    res_norm = lax.optimization_barrier(jnp.sum(residual * residual, axis=-1))
    for sweep in range(ITERS):
        image = operate(direction)
        step_len = res_norm / (lax.optimization_barrier(jnp.sum(direction * image, axis=-1)) + 1e-06)
        solution = solution + step_len[..., None] * direction
        residual = residual - step_len[..., None] * image
        new_norm = lax.optimization_barrier(jnp.sum(residual * residual, axis=-1))
        direction = residual + (new_norm / (res_norm + 1e-06))[..., None] * direction
        res_norm = new_norm
    from_state = jnp.einsum('chde,cbhe->cbhd', value_entry, solution, precision=HIGHEST) * valid
    in_block = jnp.einsum('chbi,cihd->cbhd', block_scores(solution), value_rows, preferred_element_type=jnp.float32)
    return from_state + in_block

def reference(qkv, lengths, reg):
    queries = normalize(qkv[:, 0])
    key_rows = normalize(qkv[:, 1]).astype(jnp.bfloat16)
    value_rows = qkv[:, 2]
    starts, start_mark, segment = doc_marks(lengths, 0, TOKENS)
    block_len = math.gcd(TOK_DEV, 256)
    block_count = TOKENS // block_len
    shape = (block_count, block_len, HEADS, HD)
    inputs = (queries.reshape(shape), key_rows.reshape(shape), value_rows.reshape(shape), segment.reshape(block_count, block_len), start_mark.reshape(block_count, block_len))

    def advance(carried, pieces):
        key_state, value_state = carried
        query_block, key_block, value_block, segment_block, mark_block = pieces
        result = solve_blocks(query_block[None], key_block[None], value_block[None], segment_block[None], mark_block[None], key_state[None], value_state[None], reg)[0]
        reset_flag, key_sum, value_sum = block_sums(key_block[None], value_block[None], segment_block[None], mark_block[None])
        keep = 1.0 - reset_flag[0]
        return ((keep * key_state + key_sum[0], keep * value_state + value_sum[0]), result)
    zeros = jnp.zeros((HEADS, HD, HD), jnp.float32)
    unused, results = lax.scan(advance, (zeros, zeros), inputs)
    return results.reshape(TOKENS, HEADS, HD).astype(jnp.bfloat16)
```

```python
import functools
import math

import jax
import jax.numpy as jnp
from jax import lax
from jax.experimental import pallas as pl
from jax.experimental.pallas import tpu as pltpu
from jax.sharding import PartitionSpec as P

ITERS = 10
BLOCK = 256
HD = 128
F32 = jnp.float32
BF = jnp.bfloat16


def dot(a, b):
    return lax.dot_general(a, b, (((1,), (0,)), ((), ())), preferred_element_type=F32)


def doc_of(info, place):
    doc = jnp.zeros_like(place)
    for j in range(info.shape[0] - 1):
        doc = doc + (place >= info[1 + j]).astype(jnp.int32)
    return doc


def sums_kernel(head_count, info, k_ref, v_ref, prefix_ref, total_ref):
    first = info[0]
    blocks = k_ref.shape[0] // 2
    last_docs = [doc_of(info, first + (b + 1) * BLOCK - 1) for b in range(blocks)]
    lanes = lax.broadcasted_iota(jnp.int32, (1, BLOCK), 1)
    for h in range(head_count):
        key_sums, value_sums = [], []
        for b in range(blocks):
            tail = (doc_of(info, first + b * BLOCK + lanes) == last_docs[b]).astype(F32).astype(BF)
            k = k_ref[2 * b : 2 * b + 2, h].reshape(BLOCK, HD)
            v = v_ref[2 * b : 2 * b + 2, h].reshape(BLOCK, HD)
            key_sums.append(dot(k.T * tail, k))
            value_sums.append(dot(v.T * tail, k))
        for which, sums in enumerate((key_sums, value_sums)):
            running = jnp.zeros((HD, HD), F32)
            for b in range(blocks):
                prefix_ref[b, h, which] = running
                if b == 0:
                    running = sums[0]
                else:
                    same = (last_docs[b] == last_docs[b - 1]).astype(F32)
                    running = same * running + sums[b]
            total_ref[h, which] = running.astype(total_ref.dtype)


def sums_call(info, k, v):
    head_count = k.shape[1]
    blocks = k.shape[0] // 2
    return pl.pallas_call(
        functools.partial(sums_kernel, head_count),
        grid_spec=pltpu.PrefetchScalarGridSpec(
            num_scalar_prefetch=1,
            grid=(1,),
            in_specs=[pl.BlockSpec(k.shape, lambda i, *_: (0, 0, 0, 0))] * 2,
            out_specs=[
                pl.BlockSpec((blocks, head_count, 2, HD, HD), lambda i, *_: (0, 0, 0, 0, 0)),
                pl.BlockSpec((head_count, 2, HD, HD), lambda i, *_: (0, 0, 0, 0)),
            ],
        ),
        out_shape=[
            jax.ShapeDtypeStruct((blocks, head_count, 2, HD, HD), F32),
            jax.ShapeDtypeStruct((head_count, 2, HD, HD), BF),
        ],
        name="block_sums",
    )(info, k, v)


def solve_kernel(
    head_count, info, reg_ref, q_ref, k_ref, v_ref, prefix_ref, entry_ref, out_ref,
    lhs, key_t, same, valid, direction, residual, solution, norm,
):
    b = pl.program_id(0)
    first = info[0]
    start = first + b * BLOCK
    before = doc_of(info, start - 1)
    carry = (doc_of(info, first - 1) == before).astype(F32)
    lane = start + lax.broadcasted_iota(jnp.int32, (1, BLOCK), 1)
    row = start + lax.broadcasted_iota(jnp.int32, (BLOCK, 1), 0)
    lane_doc = doc_of(info, lane)
    valid[...] = (lane_doc == before).astype(F32)
    same[...] = ((doc_of(info, row) == lane_doc) & (row <= lane)).astype(F32).astype(BF)
    for h in range(head_count):
        k = k_ref[:, h].reshape(BLOCK, HD)
        state = prefix_ref[0, h, 0] + carry * entry_ref[h, 0].astype(F32)
        high = state.astype(BF)
        lhs[h, 0:BLOCK] = k
        lhs[h, BLOCK : BLOCK + HD] = high
        lhs[h, BLOCK + HD : BLOCK + 2 * HD] = (state - high.astype(F32)).astype(BF)
        key_t[h] = k.T
        q = q_ref[:, h].reshape(BLOCK, HD).T.astype(F32)
        q = q * lax.rsqrt(jnp.mean(q * q, axis=0, keepdims=True) + 1e-06) / math.sqrt(HD)
        direction[h] = q
        residual[h] = q
        solution[h] = jnp.zeros_like(q)
        norm[h] = jnp.sum(q * q, axis=0, keepdims=True)

    def iterate(_, carried):
        held = []
        for h in range(head_count):
            p = direction[h]
            high = p.astype(BF)
            low = (p - high.astype(F32)).astype(BF)
            full = dot(lhs[h], high)
            rest = dot(lhs[h, BLOCK : BLOCK + HD], low)
            score = full[0:BLOCK].astype(BF) * same[...]
            held.append((p, full[BLOCK : BLOCK + HD] + full[BLOCK + HD :] + rest, score))
        for h in range(head_count):
            p, from_state, score = held[h]
            image = from_state * valid[...] + dot(key_t[h], score) + reg_ref[h] * p
            old = norm[h]
            step = old / (jnp.sum(p * image, axis=0, keepdims=True) + 1e-06)
            solution[h] = solution[h] + step * p
            r = residual[h] - step * image
            residual[h] = r
            new = jnp.sum(r * r, axis=0, keepdims=True)
            direction[h] = r + (new / (old + 1e-06)) * p
            norm[h] = new
        return carried

    lax.fori_loop(0, ITERS, iterate, 0)
    for h in range(head_count):
        x = solution[h]
        high = x.astype(BF)
        low = (x - high.astype(F32)).astype(BF)
        state = prefix_ref[0, h, 1] + carry * entry_ref[h, 1].astype(F32)
        state_high = state.astype(BF)
        state_low = (state - state_high.astype(F32)).astype(BF)
        score = dot(lhs[h, 0:BLOCK], high).astype(BF) * same[...]
        from_state = dot(state_high, high) + dot(state_low, high) + dot(state_high, low)
        v = v_ref[:, h].reshape(BLOCK, HD)
        result = from_state * valid[...] + dot(v.T, score)
        out_ref[:, h] = result.T.astype(BF).reshape(2, HD, HD)


def solve_call(info, damping, q, k, v, prefix, entry):
    head_count = q.shape[1]
    blocks = q.shape[0] // 2
    tokens = pl.BlockSpec((2, head_count, HD, HD), lambda b, *_: (b, 0, 0, 0))
    vectors = pltpu.VMEM((head_count, HD, BLOCK), F32)
    return pl.pallas_call(
        functools.partial(solve_kernel, head_count),
        grid_spec=pltpu.PrefetchScalarGridSpec(
            num_scalar_prefetch=2,
            grid=(blocks,),
            in_specs=[
                tokens,
                tokens,
                tokens,
                pl.BlockSpec((1, head_count, 2, HD, HD), lambda b, *_: (b, 0, 0, 0, 0)),
                pl.BlockSpec((head_count, 2, HD, HD), lambda b, *_: (0, 0, 0, 0)),
            ],
            out_specs=tokens,
            scratch_shapes=[
                pltpu.VMEM((head_count, BLOCK + 2 * HD, HD), BF),
                pltpu.VMEM((head_count, HD, BLOCK), BF),
                pltpu.VMEM((BLOCK, BLOCK), BF),
                pltpu.VMEM((1, BLOCK), F32),
                vectors,
                vectors,
                vectors,
                pltpu.VMEM((head_count, 1, BLOCK), F32),
            ],
        ),
        out_shape=jax.ShapeDtypeStruct(q.shape, BF),
        name="solve_blocks",
    )(info, damping, q, k, v, prefix, entry)


def normalize(rows):
    rows = rows.astype(F32)
    return (
        rows
        * lax.rsqrt(jnp.mean(rows * rows, axis=-1, keepdims=True) + 1e-06)
        / math.sqrt(rows.shape[-1])
    )


def body(qkv, lengths, reg):
    groups = lax.axis_size("head")
    places = lax.axis_size("ctx")
    rows, _, heads, width = qkv.shape
    mine = heads // groups
    local = rows * groups
    place = lax.axis_index("ctx")
    starts = (jnp.cumsum(lengths) - lengths).astype(jnp.int32)
    info = jnp.concatenate([jnp.reshape(place * local, (1,)).astype(jnp.int32), starts])
    damping = lax.dynamic_slice_in_dim(reg, lax.axis_index("head") * mine, mine)

    split = qkv.reshape(rows, 3, groups, mine, width)
    keys = normalize(split[:, 1]).astype(BF)
    key_value = jnp.stack([keys, split[:, 2]]).transpose(2, 0, 3, 1, 4)
    query = split[:, 0].transpose(1, 2, 0, 3)

    key_value = lax.all_to_all(key_value, "head", 0, 0, tiled=True)
    query = lax.all_to_all(query, "head", 0, 0, tiled=True)
    k, v = key_value[:, 0], key_value[:, 1]
    prefix, total = sums_call(info, k, v)

    ends = local * jnp.arange(1, places + 1, dtype=jnp.int32) - 1
    last = jnp.sum((starts[None, :] <= ends[:, None]).astype(jnp.int32), axis=1)
    order = jnp.arange(places)
    wanted = jnp.concatenate([jnp.zeros((1,), jnp.int32), last[:-1]])
    weight = ((order[None, :] < order[:, None]) & (wanted[:, None] == last[None, :])).astype(BF)
    sliced = lax.all_to_all(total.reshape(places, -1, width), "ctx", 0, 0, tiled=True)
    entries = jnp.einsum("pc,crw->prw", weight, sliced, preferred_element_type=F32).astype(BF)
    entry = lax.all_to_all(entries, "ctx", 0, 0, tiled=True).reshape(total.shape)

    mixed = solve_call(info, damping, query, k, v, prefix, entry)
    mixed = lax.all_to_all(mixed, "head", 0, 0, tiled=True)
    return mixed.reshape(heads, rows, width).transpose(1, 0, 2)


def solution(mesh):
    in_specs = (P(("ctx", "head"), None, None, None), P(), P())
    out_specs = P(("ctx", "head"), None, None)
    return jax.shard_map(body, mesh=mesh, in_specs=in_specs, out_specs=out_specs, check_vma=False)
```

```python
import functools
import math

import jax
import jax.numpy as jnp
from jax import lax
from jax.experimental import pallas as pl
from jax.experimental.pallas import tpu as pltpu
from jax.sharding import PartitionSpec as P

ITERS = 10
PAIRS = ((0, 1), (3, 2))
BLOCK = 256
HD = 128
NX = 4
NY = 4
NZ = 8
PER = 4
F32 = jnp.float32
BF = jnp.bfloat16
VMEM = pl.BlockSpec(memory_space=pltpu.VMEM)
SMEM = pl.BlockSpec(memory_space=pltpu.SMEM)


def dot(a, b):
    return lax.dot_general(a, b, (((1,), (0,)), ((), ())), preferred_element_type=F32)


def call(kernel, outs, name, scratch=(), scalars=2, flops=0):
    def run(*args):
        moved = sum(math.prod(s) * d.dtype.itemsize for s, d in ((a.shape, a) for a in args))
        return pl.pallas_call(
            kernel,
            in_specs=[SMEM] * scalars + [VMEM] * (len(args) - scalars),
            out_specs=jax.tree.map(lambda _: VMEM, outs),
            out_shape=outs,
            scratch_shapes=list(scratch),
            cost_estimate=pl.CostEstimate(flops=flops, bytes_accessed=moved, transcendentals=0),
            name=name,
        )(*args)

    return run


def spot(info):
    return info[0] // 2, info[0] % 2, info[1] // NZ, info[1] % NZ


def doc_of(lengths, place):
    doc = jnp.zeros_like(place)
    start = jnp.int32(0)
    for j in range(lengths.shape[0]):
        doc = doc + (place >= start).astype(jnp.int32)
        start = start + lengths[j]
    return doc


def places_of(info, axis):
    x, core, _, _ = spot(info)
    shape = (1, BLOCK) if axis == 1 else (BLOCK, 1)
    entry = lax.broadcasted_iota(jnp.int32, shape, axis)
    half = BLOCK // 2
    base = (info[1] * NX + x) * BLOCK
    return base + jnp.where(entry < half, entry + core * half, entry - core * half)


def diagonals():
    row = lax.broadcasted_iota(jnp.int32, (HD, HD), 0)
    lane = lax.broadcasted_iota(jnp.int32, (HD, HD), 1)
    return row == lane, lane == lax.rem(row + 1, HD)


def rounded(state):
    eye, beside = diagonals()
    whole = state + pltpu.roll(state, HD - 1, 1)
    rest = whole - whole.astype(BF).astype(F32)
    return jnp.where(eye, whole, jnp.where(beside, pltpu.roll(rest, 1, 1), state)).astype(BF)


def started(state):
    _, beside = diagonals()
    return jnp.where(beside, 0.0, state)


def pack_kernel(info, x_ref, kv_own, q_own, kv_other, q_other, stage):
    _, core, _, _ = spot(info)
    rows = x_ref.shape[0]
    for kind in range(3):
        for other in range(2):
            half = core if other == 0 else 1 - core
            first = pl.multiple_of(kind * 32 + half * 16, 16)
            part = x_ref[:, pl.ds(first, 16), :].astype(F32)
            if kind == 1:
                part = (
                    part
                    * lax.rsqrt(jnp.mean(part * part, axis=-1, keepdims=True) + 1e-06)
                    / math.sqrt(HD)
                )
            stage[...] = part.reshape(rows * 16, HD)
            for h in range(16):
                tile = stage[pl.ds(h, rows, stride=16), :].astype(BF)
                if kind == 0:
                    (q_own, q_other)[other][h] = tile
                else:
                    (kv_own, kv_other)[other][kind - 1, h] = tile


def sums_kernel(info, lengths, own, other, out0, out1, out2, out3):
    x, _, _, _ = spot(info)
    place = places_of(info, 1)
    last = (info[1] * NX + x + 1) * BLOCK - 1
    tail = (doc_of(lengths, place) == doc_of(lengths, last)).astype(F32).astype(BF)
    for shift, out in enumerate((out0, out1, out2, out3)):
        for j in range(PER):
            h = lax.rem(x + shift, NX) * PER + j
            k = jnp.concatenate([own[0, h], other[0, h]], axis=0)
            v = jnp.concatenate([own[1, h], other[1, h]], axis=0)
            out[j, 0] = rounded(started(dot(k.T * tail, k)))
            out[j, 1] = dot(v.T * tail, k).astype(BF)


def block_order(info, parts, stage):
    x, _, _, _ = spot(info)
    for shift, part in enumerate(parts):
        stage[lax.rem(x - shift + NX, NX)] = part[...]


def totals_kernel(info, lengths, p0, p1, p2, p3, *rest):
    outs, (stage, ready) = rest[:NZ], rest[NZ:]
    _, _, _, z = spot(info)
    block_order(info, (p0, p1, p2, p3), stage)
    first = info[1] * NX * BLOCK
    docs = [doc_of(lengths, first + (b + 1) * BLOCK - 1) for b in range(NX)]
    for j in range(PER):
        for which in range(2):
            total = jnp.zeros((HD, HD), F32)
            for b in range(NX):
                keep = (docs[b] == docs[NX - 1]).astype(F32)
                total = total + keep * stage[b, j, which].astype(F32)
            ready[2 * j + which] = rounded(total) if which == 0 else total.astype(BF)
    for shift, out in enumerate(outs):
        out[...] = ready[lax.rem(z + shift, NZ)]


def row_order(info, parts, stage):
    _, _, _, z = spot(info)
    for shift, part in enumerate(parts):
        stage[lax.rem(z - shift + NZ, NZ)] = part[...]


def row_docs(info, lengths):
    _, _, y, _ = spot(info)
    width = NX * BLOCK
    return [doc_of(lengths, (y * NZ + place + 1) * width - 1) for place in range(-1, NZ)]


def row_kernel(info, lengths, *rest):
    parts, (out,) = rest[:NZ], rest[NZ : NZ + 1]
    stage = rest[NZ + 1]
    row_order(info, parts, stage)
    docs = row_docs(info, lengths)
    total = jnp.zeros((HD, HD), F32)
    for place in range(NZ):
        keep = (docs[place + 1] == docs[NZ]).astype(F32)
        total = total + keep * stage[place].astype(F32)
    out[...] = total


def entries_kernel(info, lengths, *rest):
    parts, (one, two), outs, (stage, ready) = rest[:NZ], rest[NZ : NZ + 2], rest[NZ + 2 : -2], rest[-2:]
    _, _, y, z = spot(info)
    row_order(info, parts, stage)
    docs = row_docs(info, lengths)
    span = NZ * NX * BLOCK
    through = (doc_of(lengths, (y - 1) * span - 1) == docs[0]).astype(F32)
    carry = one[...] + through * two[...]
    symmetric = z % 2 == 0
    running = carry
    for place in range(NZ):
        ready[place] = jnp.where(symmetric, rounded(running), running.astype(BF))
        same = (docs[place + 1] == docs[place]).astype(F32)
        running = same * running + stage[place].astype(F32)
    for shift, out in enumerate(outs):
        out[...] = ready[lax.rem(z + shift, NZ)]


def states_kernel(info, lengths, p0, p1, p2, p3, *rest):
    parts, outs, (stage, entry, ready) = rest[:NZ], rest[NZ : NZ + NX], rest[NZ + NX :]
    x, _, _, z = spot(info)
    block_order(info, (p0, p1, p2, p3), stage)
    row_order(info, parts, entry)
    first = info[1] * NX * BLOCK
    docs = [doc_of(lengths, first + b * BLOCK - 1) for b in range(NX + 1)]
    for j in range(PER):
        for which in range(2):
            running = entry[2 * j + which].astype(F32)
            for b in range(NX):
                ready[b, j, which] = rounded(running) if which == 0 else running.astype(BF)
                if b < NX - 1:
                    same = (docs[b + 1] == docs[b]).astype(F32)
                    running = same * running + stage[b, j, which].astype(F32)
    for shift, out in enumerate(outs):
        out[...] = ready[lax.rem(x + shift, NX)]


def solve_kernel(
    shifts, info, lengths, reg, kv_own, kv_other, q_own, q_other, s0, s1, out_own, out_other,
    lhs, key_t, same, valid, diagonal, direction, residual, solution, norm,
):
    x, core, _, _ = spot(info)
    before = doc_of(lengths, (info[1] * NX + x) * BLOCK - 1)
    lane = places_of(info, 1)
    row = places_of(info, 0)
    lane_doc = doc_of(lengths, lane)
    valid[...] = (lane_doc == before).astype(F32)
    same[...] = ((doc_of(lengths, row) == lane_doc) & (row <= lane)).astype(F32).astype(BF)
    eye, beside = diagonals()
    count = 2 * PER

    def head(i):
        return lax.rem(x - shifts[i // PER] + NX, NX) * PER + i % PER

    def state(i, which):
        return (s0, s1)[i // PER][i % PER, which]

    for i in range(count):
        h = head(i)
        k = jnp.concatenate([kv_own[0, h], kv_other[0, h]], axis=0)
        keys = state(i, 0).astype(F32)
        mirrored = keys.T
        lhs[i, 0:BLOCK] = k
        lhs[i, BLOCK:] = jnp.where(eye, 0.0, jnp.where(beside, mirrored, keys)).astype(BF)
        key_t[i] = k.T
        middle = jnp.sum(jnp.where(eye | beside, keys, 0.0), axis=1, keepdims=True)
        diagonal[i] = middle * valid[...] + reg[core * 16 + h]
        q = jnp.concatenate([q_own[h], q_other[h]], axis=0).T.astype(F32)
        q = q * lax.rsqrt(jnp.mean(q * q, axis=0, keepdims=True) + 1e-06) / math.sqrt(HD)
        direction[i] = q
        residual[i] = q
        solution[i] = jnp.zeros_like(q)
        norm[i] = jnp.sum(q * q, axis=0, keepdims=True)

    def apply(i):
        full = dot(lhs[i], direction[i].astype(BF))
        return full[BLOCK:], full[0:BLOCK].astype(BF) * same[...]

    def update(i, from_state, score):
        p = direction[i]
        image = from_state * valid[...] + dot(key_t[i], score) + diagonal[i] * p
        old = norm[i]
        step = old / (jnp.sum(p * image, axis=0, keepdims=True) + 1e-06)
        solution[i] = solution[i] + step * p
        r = residual[i] - step * image
        residual[i] = r
        new = jnp.sum(r * r, axis=0, keepdims=True)
        direction[i] = r + (new / (old + 1e-06)) * p
        norm[i] = new

    def iterate(_, carried):
        held = {}
        for i in range(count + 2):
            if i < count:
                held[i] = apply(i)
            if i >= 2:
                update(i - 2, *held.pop(i - 2))
        return carried

    lax.fori_loop(0, ITERS, iterate, 0)
    for i in range(count):
        h = head(i)
        u = solution[i]
        high = u.astype(BF)
        low = (u - high.astype(F32)).astype(BF)
        score = dot(lhs[i, 0:BLOCK], high).astype(BF) * same[...]
        values = state(i, 1)
        from_state = dot(values, high) + dot(values, low)
        v = jnp.concatenate([kv_own[1, h], kv_other[1, h]], axis=0)
        result = (from_state * valid[...] + dot(v.T, score)).T.astype(BF)
        out_own[i] = result[0 : BLOCK // 2]
        out_other[i] = result[BLOCK // 2 :]


def unpack_kernel(info, own0, own1, other0, other1, out_ref, stage):
    x, core, _, _ = spot(info)
    rows = out_ref.shape[0]
    for other in range(2):
        for i in range(16):
            shift = PAIRS[i // 8][i // PER % 2]
            h = lax.rem(x - shift + NX, NX) * PER + i % PER
            part = ((own0, own1), (other0, other1))[other][i // 8]
            stage[pl.ds(h, rows, stride=16), :] = part[i % 8].astype(F32)
        half = core if other == 0 else 1 - core
        first = pl.multiple_of(half * 16, 16)
        out_ref[:, pl.ds(first, 16), :] = stage[...].reshape(rows, 16, HD).astype(BF)


def body(qkv, lengths, reg):
    rows, _, heads, width = qkv.shape
    half = heads // 2
    index = jnp.arange(2, dtype=jnp.int32)
    info = jnp.where(index == 0, lax.axis_index("head"), lax.axis_index("ctx")).astype(jnp.int32)

    def array(shape, dtype=BF):
        return jax.ShapeDtypeStruct(shape, dtype)

    def swap(a):
        return lax.ppermute(a, "head", [(i, i ^ 1) for i in range(2 * NX)])

    def along_x(a, shift):
        return lax.ppermute(
            a, "head", [(i, (i + 2 * shift) % (2 * NX)) for i in range(2 * NX)]
        )

    def along_z(a, shift):
        return lax.ppermute(
            a, "ctx", [(y * NZ + z, y * NZ + (z + shift) % NZ) for y in range(NY) for z in range(NZ)]
        )

    def along_y(a, shift):
        return lax.ppermute(
            a, "ctx", [(y * NZ + z, (y + shift) * NZ + z) for y in range(NY - shift) for z in range(NZ)]
        )

    def spread(parts, move):
        return [parts[0]] + [move(part, shift) for shift, part in enumerate(parts) if shift]

    kv, q = array((2, half, rows, width)), array((half, rows, width))
    kv_own, q_own, kv_send, q_send = call(
        pack_kernel, [kv, q, kv, q], "pack", [pltpu.VMEM((rows * half, width), F32)], scalars=1
    )(info, qkv.reshape(rows, 3 * heads, width))
    kv_other = swap(kv_send)
    q_other = swap(q_send)

    states = array((PER, 2, width, width))
    parts = call(sums_kernel, [states] * NX, "block_sums")(info, lengths, kv_own, kv_other)
    parts = spread(parts, along_x)

    square = array((width, width))
    stage = pltpu.VMEM((NX, PER, 2, width, width), BF)
    squares = pltpu.VMEM((NZ, width, width), BF)
    slices = call(totals_kernel, [square] * NZ, "ctx_totals", [stage, squares])(
        info, lengths, *parts
    )
    slices = spread(slices, along_z)
    (ending,) = call(row_kernel, [array((width, width), F32)], "row_total", [squares])(
        info, lengths, *slices
    )
    carried = [along_y(ending, 1), along_y(ending, 2)]
    entries = call(entries_kernel, [square] * NZ, "entries", [squares, squares])(
        info, lengths, *slices, *carried
    )
    entries = spread(entries, along_z)
    before = call(states_kernel, [states] * NX, "block_states", [stage, squares, stage])(
        info, lengths, *parts, *entries
    )
    before = spread(before, along_x)

    vectors = pltpu.VMEM((2 * PER, width, BLOCK), F32)
    result = array((2 * PER, rows, width))
    own, other = [], []
    for shifts in PAIRS:
        mine, others = call(
            functools.partial(solve_kernel, shifts),
            [result, result],
            "solve",
            [
                pltpu.VMEM((2 * PER, BLOCK + width, width), BF),
                pltpu.VMEM((2 * PER, width, BLOCK), BF),
                pltpu.VMEM((BLOCK, BLOCK), BF),
                pltpu.VMEM((1, BLOCK), F32),
                vectors,
                vectors,
                vectors,
                vectors,
                pltpu.VMEM((2 * PER, 1, BLOCK), F32),
            ],
            scalars=3,
            flops=10**10,
        )(info, lengths, reg, kv_own, kv_other, q_own, q_other, before[shifts[0]], before[shifts[1]])
        own.append(mine)
        other.append(swap(others))
    return call(
        unpack_kernel,
        array((rows, heads, width)),
        "unpack",
        [pltpu.VMEM((rows * half, width), F32)],
        scalars=1,
    )(info, *own, *other)


def solution(mesh):
    in_specs = (P(("ctx", "head"), None, None, None), P(), P())
    out_specs = P(("ctx", "head"), None, None)
    return jax.shard_map(body, mesh=mesh, in_specs=in_specs, out_specs=out_specs, check_vma=False)
```

```python
import functools
import math

import jax
import jax.numpy as jnp
from jax import lax
from jax.experimental import pallas as pl
from jax.experimental.pallas import tpu as pltpu
from jax.sharding import PartitionSpec as P

ITERS = 10
GROUPS = ((0,), (1, 3), (2,))
BLOCK = 256
HD = 128
NX = 4
NY = 4
NZ = 8
PER = 4
F32 = jnp.float32
BF = jnp.bfloat16
VMEM = pl.BlockSpec(memory_space=pltpu.VMEM)
SMEM = pl.BlockSpec(memory_space=pltpu.SMEM)


def dot(a, b):
    return lax.dot_general(a, b, (((1,), (0,)), ((), ())), preferred_element_type=F32)


def call(kernel, outs, name, scratch=(), scalars=2, flops=0, limit=16):
    def run(*args):
        moved = sum(math.prod(s) * d.dtype.itemsize for s, d in ((a.shape, a) for a in args))
        return pl.pallas_call(
            kernel,
            in_specs=[SMEM] * scalars + [VMEM] * (len(args) - scalars),
            out_specs=jax.tree.map(lambda _: VMEM, outs),
            out_shape=outs,
            scratch_shapes=list(scratch),
            cost_estimate=pl.CostEstimate(flops=flops, bytes_accessed=moved, transcendentals=0),
            compiler_params=pltpu.CompilerParams(vmem_limit_bytes=limit << 20),
            name=name,
        )(*args)

    return run


def spot(info):
    return info[0] // 2, info[0] % 2, info[1] // NZ, info[1] % NZ


def doc_of(lengths, place):
    doc = jnp.zeros_like(place)
    start = jnp.int32(0)
    for j in range(lengths.shape[0]):
        doc = doc + (place >= start).astype(jnp.int32)
        start = start + lengths[j]
    return doc


def places_of(info, axis):
    x, core, _, _ = spot(info)
    shape = (1, BLOCK) if axis == 1 else (BLOCK, 1)
    entry = lax.broadcasted_iota(jnp.int32, shape, axis)
    half = BLOCK // 2
    base = (info[1] * NX + x) * BLOCK
    return base + jnp.where(entry < half, entry + core * half, entry - core * half)


def diagonals():
    row = lax.broadcasted_iota(jnp.int32, (HD, HD), 0)
    lane = lax.broadcasted_iota(jnp.int32, (HD, HD), 1)
    return row == lane, lane == lax.rem(row + 1, HD)


def rounded(state):
    eye, beside = diagonals()
    whole = state + pltpu.roll(state, HD - 1, 1)
    rest = whole - whole.astype(BF).astype(F32)
    return jnp.where(eye, whole, jnp.where(beside, pltpu.roll(rest, 1, 1), state)).astype(BF)


def started(state):
    _, beside = diagonals()
    return jnp.where(beside, 0.0, state)


def pack_kernel(info, x_ref, kv_own, q_own, kv_other, q_other, stage):
    _, core, _, _ = spot(info)
    rows = x_ref.shape[0]
    for kind in range(3):
        for other in range(2):
            half = core if other == 0 else 1 - core
            first = pl.multiple_of(kind * 32 + half * 16, 16)
            part = x_ref[:, pl.ds(first, 16), :].astype(F32)
            if kind == 1:
                part = (
                    part
                    * lax.rsqrt(jnp.mean(part * part, axis=-1, keepdims=True) + 1e-06)
                    / math.sqrt(HD)
                )
            stage[...] = part.reshape(rows * 16, HD)
            for h in range(16):
                tile = stage[pl.ds(h, rows, stride=16), :].astype(BF)
                if kind == 0:
                    (q_own, q_other)[other][h] = tile
                else:
                    (kv_own, kv_other)[other][kind - 1, h] = tile


def sums_kernel(shift, info, lengths, own, other, out):
    x, _, _, _ = spot(info)
    place = places_of(info, 1)
    last = (info[1] * NX + x + 1) * BLOCK - 1
    tail = (doc_of(lengths, place) == doc_of(lengths, last)).astype(F32).astype(BF)
    for j in range(PER):
        h = lax.rem(x + shift, NX) * PER + j
        k = jnp.concatenate([own[0, h], other[0, h]], axis=0)
        v = jnp.concatenate([own[1, h], other[1, h]], axis=0)
        out[j, 0] = rounded(started(dot(k.T * tail, k)))
        out[j, 1] = dot(v.T * tail, k).astype(BF)


def weighted(out, terms):
    for j in range(PER):
        for which in range(2):
            total = jnp.zeros((HD, HD), F32)
            for weight, part in terms:
                total = total + weight * part[j, which].astype(F32)
            out[j, which] = rounded(total) if which == 0 else total.astype(BF)


def block_docs(info, lengths):
    first = info[1] * NX * BLOCK
    return [doc_of(lengths, first + b * BLOCK - 1) for b in range(NX + 1)]


def pick(values, place):
    out = values[0]
    for i in range(1, len(values)):
        out = jnp.where(place == i, values[i], out)
    return out


def totals_kernel(info, lengths, p0, p1, p2, p3, out):
    x, _, _, _ = spot(info)
    docs = block_docs(info, lengths)
    terms = []
    for shift, part in enumerate((p0, p1, p2, p3)):
        doc = pick(docs[1:], lax.rem(x - shift + NX, NX))
        terms.append(((doc == docs[NX]).astype(F32), part))
    weighted(out, terms)


def entries_kernel(info, lengths, parts, out):
    count, rows, _ = parts.shape
    width = NX * BLOCK
    docs = [doc_of(lengths, c * width - 1) for c in range(count + 1)]
    per = HD // rows
    symmetric = (info[1] // per) % 2 == 0
    row = (info[1] % per) * rows + lax.broadcasted_iota(jnp.int32, (rows, HD), 0)
    lane = lax.broadcasted_iota(jnp.int32, (rows, HD), 1)
    eye = (row == lane) & symmetric
    beside = (lane == lax.rem(row + 1, HD)) & symmetric
    running = jnp.zeros((rows, HD), F32)
    for c in range(count):
        whole = running + pltpu.roll(running, HD - 1, 1)
        rest = pltpu.roll(whole - whole.astype(BF).astype(F32), 1, 1)
        out[c] = jnp.where(eye, whole, jnp.where(beside, rest, running)).astype(BF)
        same = (docs[c + 1] == docs[c]).astype(F32)
        running = same * running + parts[c].astype(F32)


def states_kernel(shift, info, lengths, p0, p1, p2, p3, entry, out):
    x, _, _, _ = spot(info)
    docs = block_docs(info, lengths)
    mine = lax.rem(x + shift, NX)
    wanted = pick(docs[:NX], mine)
    terms = [((docs[0] == wanted).astype(F32), entry)]
    for back, part in enumerate((p0, p1, p2, p3)):
        b = lax.rem(x - back + NX, NX)
        terms.append((((b < mine) & (pick(docs[1:], b) == wanted)).astype(F32), part))
    weighted(out, terms)


def solve_kernel(
    shifts, info, lengths, reg, kv_own, kv_other, q_own, q_other, *rest,
):
    states, rest = rest[: len(shifts)], rest[len(shifts) :]
    out_own, out_other, lhs, key_t, same, valid = rest[:6]
    diagonal, direction, residual, solution, norm = rest[6:]
    x, core, _, _ = spot(info)
    before = doc_of(lengths, (info[1] * NX + x) * BLOCK - 1)
    lane = places_of(info, 1)
    row = places_of(info, 0)
    lane_doc = doc_of(lengths, lane)
    valid[...] = (lane_doc == before).astype(F32)
    same[...] = ((doc_of(lengths, row) == lane_doc) & (row <= lane)).astype(F32).astype(BF)
    eye, beside = diagonals()
    count = len(shifts) * PER

    def head(i):
        return lax.rem(x - shifts[i // PER] + NX, NX) * PER + i % PER

    def state(i, which):
        return states[i // PER][i % PER, which]

    for i in range(count):
        h = head(i)
        k = jnp.concatenate([kv_own[0, h], kv_other[0, h]], axis=0)
        keys = state(i, 0).astype(F32)
        mirrored = keys.T
        lhs[i, 0:BLOCK] = k
        lhs[i, BLOCK:] = jnp.where(eye, 0.0, jnp.where(beside, mirrored, keys)).astype(BF)
        key_t[i] = k.T
        middle = jnp.sum(jnp.where(eye | beside, keys, 0.0), axis=1, keepdims=True)
        diagonal[i] = middle * valid[...] + reg[core * 16 + h]
        q = jnp.concatenate([q_own[h], q_other[h]], axis=0).T.astype(F32)
        q = q * lax.rsqrt(jnp.mean(q * q, axis=0, keepdims=True) + 1e-06) / math.sqrt(HD)
        direction[i] = q
        residual[i] = q
        solution[i] = jnp.zeros_like(q)
        norm[i] = jnp.sum(q * q, axis=0, keepdims=True)

    def apply(i):
        full = dot(lhs[i], direction[i].astype(BF))
        return full[BLOCK:], full[0:BLOCK].astype(BF) * same[...]

    def update(i, from_state, score):
        p = direction[i]
        image = from_state * valid[...] + dot(key_t[i], score) + diagonal[i] * p
        old = norm[i]
        step = old / (jnp.sum(p * image, axis=0, keepdims=True) + 1e-06)
        solution[i] = solution[i] + step * p
        r = residual[i] - step * image
        residual[i] = r
        new = jnp.sum(r * r, axis=0, keepdims=True)
        direction[i] = r + (new / (old + 1e-06)) * p
        norm[i] = new

    def iterate(_, carried):
        held = {}
        for i in range(count + 2):
            if i < count:
                held[i] = apply(i)
            if i >= 2:
                update(i - 2, *held.pop(i - 2))
        return carried

    lax.fori_loop(0, ITERS, iterate, 0)
    for i in range(count):
        h = head(i)
        u = solution[i]
        high = u.astype(BF)
        low = (u - high.astype(F32)).astype(BF)
        score = dot(lhs[i, 0:BLOCK], high).astype(BF) * same[...]
        values = state(i, 1)
        from_state = dot(values, high) + dot(values, low)
        v = jnp.concatenate([kv_own[1, h], kv_other[1, h]], axis=0)
        result = (from_state * valid[...] + dot(v.T, score)).T.astype(BF)
        out_own[i] = result[0 : BLOCK // 2]
        out_other[i] = result[BLOCK // 2 :]


def unpack_kernel(info, *rest):
    parts, (out_ref, stage) = rest[:-2], rest[-2:]
    x, core, _, _ = spot(info)
    rows = out_ref.shape[0]
    for other in range(2):
        for g, shifts in enumerate(GROUPS):
            part = parts[2 * g + other]
            for i in range(len(shifts) * PER):
                h = lax.rem(x - shifts[i // PER] + NX, NX) * PER + i % PER
                stage[pl.ds(h, rows, stride=16), :] = part[i].astype(F32)
        half = core if other == 0 else 1 - core
        first = pl.multiple_of(half * 16, 16)
        out_ref[:, pl.ds(first, 16), :] = stage[...].reshape(rows, 16, HD).astype(BF)


def body(qkv, lengths, reg):
    rows, _, heads, width = qkv.shape
    half = heads // 2
    index = jnp.arange(2, dtype=jnp.int32)
    info = jnp.where(index == 0, lax.axis_index("head"), lax.axis_index("ctx")).astype(jnp.int32)

    def array(shape, dtype=BF):
        return jax.ShapeDtypeStruct(shape, dtype)

    def swap(a):
        return lax.ppermute(a, "head", [(i, i ^ 1) for i in range(2 * NX)])

    def along_x(a, shift):
        return lax.ppermute(
            a, "head", [(i, (i + 2 * shift) % (2 * NX)) for i in range(2 * NX)]
        )

    kv, q = array((2, half, rows, width)), array((half, rows, width))
    kv_own, q_own, kv_send, q_send = call(
        pack_kernel, [kv, q, kv, q], "pack", [pltpu.VMEM((rows * half, width), F32)], scalars=1
    )(info, qkv.reshape(rows, 3 * heads, width))
    kv_other = swap(kv_send)
    q_other = swap(q_send)

    states = array((PER, 2, width, width))
    order = (2, 1, 3, 0)
    parts = [None] * NX
    for shift in order:
        part = call(functools.partial(sums_kernel, shift), states, "block_sums")(
            info, lengths, kv_own, kv_other
        )
        parts[shift] = along_x(part, shift) if shift else part
    total = call(totals_kernel, states, "ctx_totals")(info, lengths, *parts)
    places = lax.axis_size("ctx")
    slices = lax.all_to_all(total.reshape(places, -1, width), "ctx", 0, 0, tiled=True)
    entries = call(entries_kernel, array(slices.shape), "entries")(info, lengths, slices)
    entry = lax.all_to_all(entries, "ctx", 0, 0, tiled=True).reshape(states.shape)
    before = [None] * NX
    for shift in order:
        part = call(functools.partial(states_kernel, shift), states, "block_states")(
            info, lengths, *parts, entry
        )
        before[shift] = along_x(part, shift) if shift else part

    results = []
    for shifts in GROUPS:
        count = len(shifts) * PER
        vectors = pltpu.VMEM((count, width, BLOCK), F32)
        result = array((count, rows, width))
        mine, others = call(
            functools.partial(solve_kernel, shifts),
            [result, result],
            "solve",
            [
                pltpu.VMEM((count, BLOCK + width, width), BF),
                pltpu.VMEM((count, width, BLOCK), BF),
                pltpu.VMEM((BLOCK, BLOCK), BF),
                pltpu.VMEM((1, BLOCK), F32),
                vectors,
                vectors,
                vectors,
                vectors,
                pltpu.VMEM((count, 1, BLOCK), F32),
            ],
            scalars=3,
            flops=10**9 * count,
            limit=24,
        )(info, lengths, reg, kv_own, kv_other, q_own, q_other, *(before[s] for s in shifts))
        results += [mine, swap(others)]
    return call(
        unpack_kernel,
        array((rows, heads, width)),
        "unpack",
        [pltpu.VMEM((rows * half, width), F32)],
        scalars=1,
    )(info, *results)


def solution(mesh):
    in_specs = (P(("ctx", "head"), None, None, None), P(), P())
    out_specs = P(("ctx", "head"), None, None)
    return jax.shard_map(body, mesh=mesh, in_specs=in_specs, out_specs=out_specs, check_vma=False)
```

```python
import functools
import math

import jax
import jax.numpy as jnp
from jax import lax
from jax.experimental import pallas as pl
from jax.experimental.pallas import tpu as pltpu
from jax.sharding import PartitionSpec as P

ITERS = 10
UNROLL = 2
GROUPS = ((0,), (1, 3), (2,))
BLOCK = 256
HD = 128
NX = 4
NY = 4
NZ = 8
PER = 4
F32 = jnp.float32
BF = jnp.bfloat16
VMEM = pl.BlockSpec(memory_space=pltpu.VMEM)
SMEM = pl.BlockSpec(memory_space=pltpu.SMEM)


def dot(a, b):
    return lax.dot_general(a, b, (((1,), (0,)), ((), ())), preferred_element_type=F32)


def call(kernel, outs, name, scratch=(), scalars=2, flops=0, limit=16):
    def run(*args):
        moved = sum(math.prod(s) * d.dtype.itemsize for s, d in ((a.shape, a) for a in args))
        return pl.pallas_call(
            kernel,
            in_specs=[SMEM] * scalars + [VMEM] * (len(args) - scalars),
            out_specs=jax.tree.map(lambda _: VMEM, outs),
            out_shape=outs,
            scratch_shapes=list(scratch),
            cost_estimate=pl.CostEstimate(flops=flops, bytes_accessed=moved, transcendentals=0),
            compiler_params=pltpu.CompilerParams(vmem_limit_bytes=limit << 20),
            name=name,
        )(*args)

    return run


def spot(info):
    return info[0] // 2, info[0] % 2, info[1] // NZ, info[1] % NZ


def doc_of(lengths, place):
    doc = jnp.zeros_like(place)
    start = jnp.int32(0)
    for j in range(lengths.shape[0]):
        doc = doc + (place >= start).astype(jnp.int32)
        start = start + lengths[j]
    return doc


def places_of(info, axis):
    x, core, _, _ = spot(info)
    shape = (1, BLOCK) if axis == 1 else (BLOCK, 1)
    entry = lax.broadcasted_iota(jnp.int32, shape, axis)
    half = BLOCK // 2
    base = (info[1] * NX + x) * BLOCK
    return base + jnp.where(entry < half, entry + core * half, entry - core * half)


def diagonals():
    row = lax.broadcasted_iota(jnp.int32, (HD, HD), 0)
    lane = lax.broadcasted_iota(jnp.int32, (HD, HD), 1)
    return row == lane, lane == lax.rem(row + 1, HD)


def rounded(state):
    eye, beside = diagonals()
    whole = state + pltpu.roll(state, HD - 1, 1)
    rest = whole - whole.astype(BF).astype(F32)
    return jnp.where(eye, whole, jnp.where(beside, pltpu.roll(rest, 1, 1), state)).astype(BF)


def started(state):
    _, beside = diagonals()
    return jnp.where(beside, 0.0, state)


def pack_kernel(keys_first, info, x_ref, out_ref, stage):
    rows = x_ref.shape[0]
    part = x_ref[...].astype(F32)
    stage[...] = part.reshape(rows * 16, HD)
    if keys_first:

        @pl.when(pl.program_id(0) == 0)
        def _():
            scale = lax.rsqrt(jnp.mean(part * part, axis=-1, keepdims=True) + 1e-06)
            stage[...] = (part * scale / math.sqrt(HD)).reshape(rows * 16, HD)

    for h in range(16):
        out_ref[0, h] = stage[pl.ds(h, rows, stride=16), :].astype(BF)


def pack(info, qkv, first, count, other):
    rows = qkv.shape[0]

    def place(g, info):
        core = info[0] % 2
        return 0, 2 * (first + g) + (1 - core if other else core), 0

    return pl.pallas_call(
        functools.partial(pack_kernel, first == 1),
        grid_spec=pltpu.PrefetchScalarGridSpec(
            num_scalar_prefetch=1,
            grid=(count,),
            in_specs=[pl.BlockSpec((rows, 16, HD), place)],
            out_specs=pl.BlockSpec((1, 16, rows, HD), lambda g, info: (g, 0, 0, 0)),
            scratch_shapes=[pltpu.VMEM((rows * 16, HD), F32)],
        ),
        out_shape=jax.ShapeDtypeStruct((count, 16, rows, HD), BF),
        compiler_params=pltpu.CompilerParams(vmem_limit_bytes=12 << 20),
        name="pack",
    )(info, qkv)


def sums_kernel(shift, info, lengths, own, other, out):
    x, _, _, _ = spot(info)
    place = places_of(info, 1)
    last = (info[1] * NX + x + 1) * BLOCK - 1
    tail = (doc_of(lengths, place) == doc_of(lengths, last)).astype(F32).astype(BF)
    for j in range(PER):
        h = lax.rem(x + shift, NX) * PER + j
        k = jnp.concatenate([own[0, h], other[0, h]], axis=0)
        v = jnp.concatenate([own[1, h], other[1, h]], axis=0)
        out[j, 0] = rounded(started(dot(k.T * tail, k)))
        out[j, 1] = dot(v.T * tail, k).astype(BF)


def weighted(out, terms):
    for j in range(PER):
        for which in range(2):
            total = jnp.zeros((HD, HD), F32)
            for weight, part in terms:
                total = total + weight * part[j, which].astype(F32)
            out[j, which] = rounded(total) if which == 0 else total.astype(BF)


def block_docs(info, lengths):
    first = info[1] * NX * BLOCK
    return [doc_of(lengths, first + b * BLOCK - 1) for b in range(NX + 1)]


def pick(values, place):
    out = values[0]
    for i in range(1, len(values)):
        out = jnp.where(place == i, values[i], out)
    return out


def totals_kernel(info, lengths, p0, p1, p2, p3, out):
    x, _, _, _ = spot(info)
    docs = block_docs(info, lengths)
    terms = []
    for shift, part in enumerate((p0, p1, p2, p3)):
        doc = pick(docs[1:], lax.rem(x - shift + NX, NX))
        terms.append(((doc == docs[NX]).astype(F32), part))
    weighted(out, terms)


def entries_kernel(info, lengths, parts, out):
    count, rows, _ = parts.shape
    width = NX * BLOCK
    docs = [doc_of(lengths, c * width - 1) for c in range(count + 1)]
    per = HD // rows
    symmetric = (info[1] // per) % 2 == 0
    row = (info[1] % per) * rows + lax.broadcasted_iota(jnp.int32, (rows, HD), 0)
    lane = lax.broadcasted_iota(jnp.int32, (rows, HD), 1)
    eye = (row == lane) & symmetric
    beside = (lane == lax.rem(row + 1, HD)) & symmetric
    running = jnp.zeros((rows, HD), F32)
    for c in range(count):
        whole = running + pltpu.roll(running, HD - 1, 1)
        rest = pltpu.roll(whole - whole.astype(BF).astype(F32), 1, 1)
        out[c] = jnp.where(eye, whole, jnp.where(beside, rest, running)).astype(BF)
        same = (docs[c + 1] == docs[c]).astype(F32)
        running = same * running + parts[c].astype(F32)


def states_kernel(shift, info, lengths, p0, p1, p2, p3, entry, out):
    x, _, _, _ = spot(info)
    docs = block_docs(info, lengths)
    mine = lax.rem(x + shift, NX)
    wanted = pick(docs[:NX], mine)
    terms = [((docs[0] == wanted).astype(F32), entry)]
    for back, part in enumerate((p0, p1, p2, p3)):
        b = lax.rem(x - back + NX, NX)
        terms.append((((b < mine) & (pick(docs[1:], b) == wanted)).astype(F32), part))
    weighted(out, terms)


def prepare_kernel(
    info, lengths, kv_own, kv_other, q_own, q_other, keys, key_t, value_t, query, same, valid
):
    x, _, _, _ = spot(info)
    before = doc_of(lengths, (info[1] * NX + x) * BLOCK - 1)
    lane = places_of(info, 1)
    row = places_of(info, 0)
    lane_doc = doc_of(lengths, lane)
    valid[...] = (lane_doc == before).astype(F32)
    same[...] = ((doc_of(lengths, row) == lane_doc) & (row <= lane)).astype(F32).astype(BF)

    def one(pair, carried):
        for h in (2 * pair, 2 * pair + 1):
            k = jnp.concatenate([kv_own[0, h], kv_other[0, h]], axis=0)
            keys[h] = k
            key_t[h] = k.T
            value_t[h] = jnp.concatenate([kv_own[1, h], kv_other[1, h]], axis=0).T
            q = jnp.concatenate([q_own[0, h], q_other[0, h]], axis=0).T.astype(F32)
            scale = lax.rsqrt(jnp.mean(q * q, axis=0, keepdims=True) + 1e-06)
            query[h] = q * scale / math.sqrt(HD)
        return carried

    lax.fori_loop(0, keys.shape[0] // 2, one, 0)


def solve_kernel(shifts, info, reg, keys, key_t, value_t, query, same, valid, *rest):
    states, rest = rest[: len(shifts)], rest[len(shifts) :]
    out_own, out_other, lhs, held_valid, diagonal, direction, residual, solution, norm = rest
    x, core, _, _ = spot(info)
    held_valid[...] = jnp.broadcast_to(valid[...], (HD, BLOCK)).astype(BF)
    eye, beside = diagonals()
    count = len(shifts) * PER
    head = [lax.rem(x - shifts[i // PER] + NX, NX) * PER + i % PER for i in range(count)]

    def state(i, which):
        return states[i // PER][i % PER, which]

    for i in range(count):
        held = state(i, 0).astype(F32)
        plain = jnp.where(eye, 0.0, jnp.where(beside, held.T, held)).astype(BF)
        lhs[i, :, 0:BLOCK] = key_t[head[i]]
        lhs[i, :, BLOCK:] = plain
        middle = jnp.sum(jnp.where(eye | beside, held, 0.0), axis=1, keepdims=True)
        diagonal[i] = middle * valid[...] + reg[core * 16 + head[i]]
        q = query[head[i]]
        direction[i] = q
        residual[i] = q
        solution[i] = jnp.zeros_like(q)
        norm[i] = jnp.sum(q * q, axis=0, keepdims=True)

    def scores(i, rounded_vector):
        return dot(keys[head[i]], rounded_vector).astype(BF) * same[...]

    def apply(i):
        p = direction[i].astype(BF)
        return jnp.concatenate([scores(i, p), p * held_valid[...]], axis=0)

    def update(i, applied):
        p = direction[i]
        image = dot(lhs[i], applied) + diagonal[i] * p
        old = norm[i]
        step = old / (jnp.sum(p * image, axis=0, keepdims=True) + 1e-06)
        solution[i] = solution[i] + step * p
        r = residual[i] - step * image
        residual[i] = r
        new = jnp.sum(r * r, axis=0, keepdims=True)
        direction[i] = r + (new / (old + 1e-06)) * p
        norm[i] = new

    def staggered(first, second, total, lag):
        held = {}
        for t in range(total + lag):
            if t < total:
                held[t] = first(t % count)
            if t >= lag:
                second((t - lag) % count, held.pop(t - lag))

    def iterate(_, carried):
        staggered(apply, update, UNROLL * count, 3)
        return carried

    def apply_last(i):
        u = solution[i]
        high = u.astype(BF)
        low = (u - high.astype(F32)).astype(BF)
        return jnp.concatenate(
            [scores(i, high), high * held_valid[...], low * held_valid[...]], axis=0
        )

    def finish(i, applied):
        values = state(i, 1)
        whole = jnp.concatenate([value_t[head[i]], values, values], axis=1)
        result = dot(whole, applied).T.astype(BF)
        out_own[i] = result[0 : BLOCK // 2]
        out_other[i] = result[BLOCK // 2 :]

    lax.fori_loop(0, ITERS // UNROLL, iterate, 0)
    staggered(apply_last, finish, count, 2)


def unpack_kernel(info, *rest):
    parts, (out_ref, stage) = rest[:-2], rest[-2:]
    x, core, _, _ = spot(info)
    rows = out_ref.shape[0]
    for other in range(2):
        for g, shifts in enumerate(GROUPS):
            part = parts[2 * g + other]
            for i in range(len(shifts) * PER):
                h = lax.rem(x - shifts[i // PER] + NX, NX) * PER + i % PER
                stage[pl.ds(h, rows, stride=16), :] = part[i].astype(F32)
        half = core if other == 0 else 1 - core
        first = pl.multiple_of(half * 16, 16)
        out_ref[:, pl.ds(first, 16), :] = stage[...].reshape(rows, 16, HD).astype(BF)


def body(qkv, lengths, reg):
    rows, _, heads, width = qkv.shape
    half = heads // 2
    index = jnp.arange(2, dtype=jnp.int32)
    info = jnp.where(index == 0, lax.axis_index("head"), lax.axis_index("ctx")).astype(jnp.int32)

    def array(shape, dtype=BF):
        return jax.ShapeDtypeStruct(shape, dtype)

    def swap(a):
        return lax.ppermute(a, "head", [(i, i ^ 1) for i in range(2 * NX)])

    def along_x(a, shift):
        return lax.ppermute(
            a, "head", [(i, (i + 2 * shift) % (2 * NX)) for i in range(2 * NX)]
        )

    def relay(a):
        ring = [(2 * x, 2 * ((x + 1) % NX)) for x in range(NX)]
        back = [(2 * x + 1, 2 * ((x - 1) % NX) + 1) for x in range(NX)]
        return lax.ppermute(a, "head", ring + back)

    flat = qkv.reshape(rows, 3 * heads, width)
    kv_other = swap(pack(info, flat, 1, 2, True))
    q_other = swap(pack(info, flat, 0, 1, True))
    kv_own = pack(info, flat, 1, 2, False)
    q_own = pack(info, flat, 0, 1, False)

    states = array((PER, 2, width, width))
    order = (2, 1, 3, 0)
    parts = [None] * NX
    own = kv_own
    for shift in order:
        if shift == 0:
            own, parts[2] = lax.optimization_barrier((own, parts[2]))
            parts[2] = relay(parts[2])
        part = call(functools.partial(sums_kernel, shift), states, "block_sums")(
            info, lengths, own, kv_other
        )
        if shift:
            part = relay(part) if shift == 2 else along_x(part, shift)
        parts[shift] = part
    columns = array((half, width, BLOCK))
    prepared = call(
        prepare_kernel,
        [
            array((half, BLOCK, width)),
            columns,
            columns,
            array(columns.shape, F32),
            array((BLOCK, BLOCK)),
            array((1, BLOCK), F32),
        ],
        "prepare",
        limit=24,
    )(info, lengths, own, kv_other, q_own, q_other)
    parts, prepared = lax.optimization_barrier((parts, prepared))
    total = call(totals_kernel, states, "ctx_totals")(info, lengths, *parts)
    places = lax.axis_size("ctx")
    slices = lax.all_to_all(total.reshape(places, -1, width), "ctx", 0, 0, tiled=True)
    entries = call(entries_kernel, array(slices.shape), "entries")(info, lengths, slices)
    entry = lax.all_to_all(entries, "ctx", 0, 0, tiled=True).reshape(states.shape)
    before = [None] * NX
    for shift in order:
        part = call(functools.partial(states_kernel, shift), states, "block_states")(
            info, lengths, *parts, entry
        )
        before[shift] = along_x(part, shift) if shift else part

    results = []
    for shifts in GROUPS:
        count = len(shifts) * PER
        vectors = pltpu.VMEM((count, width, BLOCK), F32)
        result = array((count, rows, width))
        mine, others = call(
            functools.partial(solve_kernel, shifts),
            [result, result],
            "solve",
            [
                pltpu.VMEM((count, width, BLOCK + width), BF),
                pltpu.VMEM((width, BLOCK), BF),
                vectors,
                vectors,
                vectors,
                vectors,
                pltpu.VMEM((count, 1, BLOCK), F32),
            ],
            flops=10**9 * count,
            limit=28,
        )(info, reg, *prepared, *(before[s] for s in shifts))
        results += [mine, swap(others)]
    return call(
        unpack_kernel,
        array((rows, heads, width)),
        "unpack",
        [pltpu.VMEM((rows * half, width), F32)],
        scalars=1,
    )(info, *results)


def solution(mesh):
    in_specs = (P(("ctx", "head"), None, None, None), P(), P())
    out_specs = P(("ctx", "head"), None, None)
    return jax.shard_map(body, mesh=mesh, in_specs=in_specs, out_specs=out_specs, check_vma=False)
```

```python
import functools
import math

import jax
import jax.numpy as jnp
from jax import lax
from jax.experimental import pallas as pl
from jax.experimental.pallas import tpu as pltpu
from jax.sharding import PartitionSpec as P

ITERS = 10
UNROLL = 5
GROUPS = ((0,), (1, 3), (2,))
BLOCK = 256
HD = 128
NX = 4
NY = 4
NZ = 8
PER = 4
F32 = jnp.float32
BF = jnp.bfloat16
VMEM = pl.BlockSpec(memory_space=pltpu.VMEM)
SMEM = pl.BlockSpec(memory_space=pltpu.SMEM)


def dot(a, b):
    return lax.dot_general(a, b, (((1,), (0,)), ((), ())), preferred_element_type=F32)


def call(kernel, outs, name, scratch=(), scalars=2, flops=0, limit=16):
    def run(*args):
        moved = sum(math.prod(s) * d.dtype.itemsize for s, d in ((a.shape, a) for a in args))
        return pl.pallas_call(
            kernel,
            in_specs=[SMEM] * scalars + [VMEM] * (len(args) - scalars),
            out_specs=jax.tree.map(lambda _: VMEM, outs),
            out_shape=outs,
            scratch_shapes=list(scratch),
            cost_estimate=pl.CostEstimate(flops=flops, bytes_accessed=moved, transcendentals=0),
            compiler_params=pltpu.CompilerParams(vmem_limit_bytes=limit << 20),
            name=name,
        )(*args)

    return run


def spot(info):
    return info[0] // 2, info[0] % 2, info[1] // NZ, info[1] % NZ


def doc_of(lengths, place):
    doc = jnp.zeros_like(place)
    start = jnp.int32(0)
    for j in range(lengths.shape[0]):
        doc = doc + (place >= start).astype(jnp.int32)
        start = start + lengths[j]
    return doc


def places_of(info, axis):
    x, core, _, _ = spot(info)
    shape = (1, BLOCK) if axis == 1 else (BLOCK, 1)
    entry = lax.broadcasted_iota(jnp.int32, shape, axis)
    half = BLOCK // 2
    base = (info[1] * NX + x) * BLOCK
    return base + jnp.where(entry < half, entry + core * half, entry - core * half)


def diagonals():
    row = lax.broadcasted_iota(jnp.int32, (HD, HD), 0)
    lane = lax.broadcasted_iota(jnp.int32, (HD, HD), 1)
    return row == lane, lane == lax.rem(row + 1, HD)


def rounded(state):
    eye, beside = diagonals()
    whole = state + pltpu.roll(state, HD - 1, 1)
    rest = whole - whole.astype(BF).astype(F32)
    return jnp.where(eye, whole, jnp.where(beside, pltpu.roll(rest, 1, 1), state)).astype(BF)


def started(state):
    _, beside = diagonals()
    return jnp.where(beside, 0.0, state)


def pack_kernel(keys_first, info, x_ref, out_ref, stage):
    rows = x_ref.shape[0]
    part = x_ref[...].astype(F32)
    stage[...] = part.reshape(rows * 16, HD)
    if keys_first:

        @pl.when(pl.program_id(0) == 0)
        def _():
            scale = lax.rsqrt(jnp.mean(part * part, axis=-1, keepdims=True) + 1e-06)
            stage[...] = (part * scale / math.sqrt(HD)).reshape(rows * 16, HD)

    for h in range(16):
        out_ref[0, h] = stage[pl.ds(h, rows, stride=16), :].astype(BF)


def pack(info, qkv, first, count, other):
    rows = qkv.shape[0]

    def place(g, info):
        core = info[0] % 2
        return 0, 2 * (first + g) + (1 - core if other else core), 0

    return pl.pallas_call(
        functools.partial(pack_kernel, first == 1),
        grid_spec=pltpu.PrefetchScalarGridSpec(
            num_scalar_prefetch=1,
            grid=(count,),
            in_specs=[pl.BlockSpec((rows, 16, HD), place)],
            out_specs=pl.BlockSpec((1, 16, rows, HD), lambda g, info: (g, 0, 0, 0)),
            scratch_shapes=[pltpu.VMEM((rows * 16, HD), F32)],
        ),
        out_shape=jax.ShapeDtypeStruct((count, 16, rows, HD), BF),
        compiler_params=pltpu.CompilerParams(vmem_limit_bytes=12 << 20),
        name="pack",
    )(info, qkv)


def sums_kernel(shift, info, lengths, own, other, out):
    x, _, _, _ = spot(info)
    place = places_of(info, 1)
    last = (info[1] * NX + x + 1) * BLOCK - 1
    tail = (doc_of(lengths, place) == doc_of(lengths, last)).astype(F32).astype(BF)
    for j in range(PER):
        h = lax.rem(x + shift, NX) * PER + j
        k = jnp.concatenate([own[0, h], other[0, h]], axis=0)
        v = jnp.concatenate([own[1, h], other[1, h]], axis=0)
        out[j, 0] = rounded(started(dot(k.T * tail, k)))
        out[j, 1] = dot(v.T * tail, k).astype(BF)


def weighted(out, terms):
    for j in range(PER):
        for which in range(2):
            total = jnp.zeros((HD, HD), F32)
            for weight, part in terms:
                total = total + weight * part[j, which].astype(F32)
            out[j, which] = rounded(total) if which == 0 else total.astype(BF)


def block_docs(info, lengths):
    first = info[1] * NX * BLOCK
    return [doc_of(lengths, first + b * BLOCK - 1) for b in range(NX + 1)]


def pick(values, place):
    out = values[0]
    for i in range(1, len(values)):
        out = jnp.where(place == i, values[i], out)
    return out


def totals_kernel(info, lengths, p0, p1, p2, p3, out):
    x, _, _, _ = spot(info)
    docs = block_docs(info, lengths)
    terms = []
    for shift, part in enumerate((p0, p1, p2, p3)):
        doc = pick(docs[1:], lax.rem(x - shift + NX, NX))
        terms.append(((doc == docs[NX]).astype(F32), part))
    weighted(out, terms)


def entries_kernel(info, lengths, parts, out):
    count, rows, _ = parts.shape
    width = NX * BLOCK
    docs = [doc_of(lengths, c * width - 1) for c in range(count + 1)]
    per = HD // rows
    symmetric = (info[1] // per) % 2 == 0
    row = (info[1] % per) * rows + lax.broadcasted_iota(jnp.int32, (rows, HD), 0)
    lane = lax.broadcasted_iota(jnp.int32, (rows, HD), 1)
    eye = (row == lane) & symmetric
    beside = (lane == lax.rem(row + 1, HD)) & symmetric
    running = jnp.zeros((rows, HD), F32)
    for c in range(count):
        whole = running + pltpu.roll(running, HD - 1, 1)
        rest = pltpu.roll(whole - whole.astype(BF).astype(F32), 1, 1)
        out[c] = jnp.where(eye, whole, jnp.where(beside, rest, running)).astype(BF)
        same = (docs[c + 1] == docs[c]).astype(F32)
        running = same * running + parts[c].astype(F32)


def states_kernel(shifts, info, lengths, p0, p1, p2, p3, entry, *outs):
    x, _, _, _ = spot(info)
    docs = block_docs(info, lengths)
    weights = []
    for shift in shifts:
        mine = lax.rem(x + shift, NX)
        wanted = pick(docs[:NX], mine)
        row = [(docs[0] == wanted).astype(F32)]
        for back in range(NX):
            b = lax.rem(x - back + NX, NX)
            row.append(((b < mine) & (pick(docs[1:], b) == wanted)).astype(F32))
        weights.append(row)
    for j in range(PER):
        for which in range(2):
            parts = [part[j, which].astype(F32) for part in (entry, p0, p1, p2, p3)]
            for row, out in zip(weights, outs):
                total = row[0] * parts[0]
                for weight, part in zip(row[1:], parts[1:]):
                    total = total + weight * part
                out[j, which] = rounded(total) if which == 0 else total.astype(BF)


def prepare_kernel(
    info, lengths, kv_own, kv_other, q_own, q_other, keys, key_t, value_t, query, same, valid
):
    x, _, _, _ = spot(info)
    before = doc_of(lengths, (info[1] * NX + x) * BLOCK - 1)
    lane = places_of(info, 1)
    row = places_of(info, 0)
    lane_doc = doc_of(lengths, lane)
    valid[...] = (lane_doc == before).astype(F32)
    same[...] = ((doc_of(lengths, row) == lane_doc) & (row <= lane)).astype(F32).astype(BF)

    def one(pair, carried):
        for h in (2 * pair, 2 * pair + 1):
            k = jnp.concatenate([kv_own[0, h], kv_other[0, h]], axis=0)
            keys[h] = k
            key_t[h] = k.T
            value_t[h] = jnp.concatenate([kv_own[1, h], kv_other[1, h]], axis=0).T
            q = jnp.concatenate([q_own[0, h], q_other[0, h]], axis=0).T.astype(F32)
            scale = lax.rsqrt(jnp.mean(q * q, axis=0, keepdims=True) + 1e-06)
            query[h] = q * scale / math.sqrt(HD)
        return carried

    lax.fori_loop(0, keys.shape[0] // 2, one, 0)


def solve_kernel(shifts, info, reg, keys, key_t, value_t, query, same, valid, *rest):
    states, rest = rest[: len(shifts)], rest[len(shifts) :]
    out_own, out_other, lhs, held_valid, diagonal, direction, residual, solution, norm = rest
    x, core, _, _ = spot(info)
    held_valid[...] = jnp.broadcast_to(valid[...], (HD, BLOCK)).astype(BF)
    eye, beside = diagonals()
    count = len(shifts) * PER
    head = [lax.rem(x - shifts[i // PER] + NX, NX) * PER + i % PER for i in range(count)]

    def state(i, which):
        return states[i // PER][i % PER, which]

    for i in range(count):
        held = state(i, 0).astype(F32)
        plain = jnp.where(eye, 0.0, jnp.where(beside, held.T, held)).astype(BF)
        lhs[i, :, 0:BLOCK] = key_t[head[i]]
        lhs[i, :, BLOCK:] = plain
        middle = jnp.sum(jnp.where(eye | beside, held, 0.0), axis=1, keepdims=True)
        diagonal[i] = middle * valid[...] + reg[core * 16 + head[i]]
        q = query[head[i]]
        direction[i] = q
        residual[i] = q
        solution[i] = jnp.zeros_like(q)
        norm[i] = jnp.sum(q * q, axis=0, keepdims=True)

    def scores(i, rounded_vector):
        return dot(keys[head[i]], rounded_vector).astype(BF) * same[...]

    def apply(i):
        p = direction[i].astype(BF)
        return jnp.concatenate([scores(i, p), p * held_valid[...]], axis=0)

    def update(i, applied):
        product = dot(lhs[i], applied)
        for c in (slice(0, BLOCK // 2), slice(BLOCK // 2, BLOCK)):
            p = direction[i, :, c]
            image = product[:, c] + diagonal[i, :, c] * p
            old = norm[i, :, c]
            step = old / (jnp.sum(p * image, axis=0, keepdims=True) + 1e-06)
            solution[i, :, c] = solution[i, :, c] + step * p
            r = residual[i, :, c] - step * image
            residual[i, :, c] = r
            new = jnp.sum(r * r, axis=0, keepdims=True)
            direction[i, :, c] = r + (new / (old + 1e-06)) * p
            norm[i, :, c] = new

    def staggered(first, second, total, lag):
        held = {}
        for t in range(total + lag):
            if t < total:
                held[t] = first(t % count)
            if t >= lag:
                second((t - lag) % count, held.pop(t - lag))

    def iterate(_, carried):
        staggered(apply, update, UNROLL * count, min(count, 4) - (count == 4))
        return carried

    def apply_last(i):
        u = solution[i]
        high = u.astype(BF)
        low = (u - high.astype(F32)).astype(BF)
        return jnp.concatenate(
            [scores(i, high), high * held_valid[...], low * held_valid[...]], axis=0
        )

    def finish(i, applied):
        values = state(i, 1)
        whole = jnp.concatenate([value_t[head[i]], values, values], axis=1)
        result = dot(whole, applied).T.astype(BF)
        out_own[i] = result[0 : BLOCK // 2]
        out_other[i] = result[BLOCK // 2 :]

    lax.fori_loop(0, ITERS // UNROLL, iterate, 0)
    staggered(apply_last, finish, count, 2)


def unpack_kernel(info, *rest):
    parts, (out_ref, stage) = rest[:-2], rest[-2:]
    x, core, _, _ = spot(info)
    rows = out_ref.shape[0]
    for other in range(2):
        for g, shifts in enumerate(GROUPS):
            part = parts[2 * g + other]
            for i in range(len(shifts) * PER):
                h = lax.rem(x - shifts[i // PER] + NX, NX) * PER + i % PER
                stage[pl.ds(h, rows, stride=16), :] = part[i].astype(F32)
        half = core if other == 0 else 1 - core
        first = pl.multiple_of(half * 16, 16)
        out_ref[:, pl.ds(first, 16), :] = stage[...].reshape(rows, 16, HD).astype(BF)


def body(qkv, lengths, reg):
    rows, _, heads, width = qkv.shape
    half = heads // 2
    index = jnp.arange(2, dtype=jnp.int32)
    info = jnp.where(index == 0, lax.axis_index("head"), lax.axis_index("ctx")).astype(jnp.int32)

    def array(shape, dtype=BF):
        return jax.ShapeDtypeStruct(shape, dtype)

    def swap(a):
        return lax.ppermute(a, "head", [(i, i ^ 1) for i in range(2 * NX)])

    def along_x(a, shift):
        return lax.ppermute(
            a, "head", [(i, (i + 2 * shift) % (2 * NX)) for i in range(2 * NX)]
        )

    def relay(a):
        ring = [(2 * x, 2 * ((x + 1) % NX)) for x in range(NX)]
        back = [(2 * x + 1, 2 * ((x - 1) % NX) + 1) for x in range(NX)]
        return lax.ppermute(a, "head", ring + back)

    flat = pltpu.with_memory_space_constraint(qkv.reshape(rows, 3 * heads, width), pltpu.HBM)
    kv_other = swap(pack(info, flat, 1, 2, True))
    q_other = swap(pack(info, flat, 0, 1, True))
    kv_own = pack(info, flat, 1, 2, False)
    q_own = pack(info, flat, 0, 1, False)

    states = array((PER, 2, width, width))
    order = (2, 1, 3, 0)
    parts = [None] * NX
    own = kv_own
    for shift in order:
        if shift == 0:
            own, parts[2] = lax.optimization_barrier((own, parts[2]))
            parts[2] = relay(parts[2])
        part = call(functools.partial(sums_kernel, shift), states, "block_sums")(
            info, lengths, own, kv_other
        )
        if shift:
            part = relay(part) if shift == 2 else along_x(part, shift)
        parts[shift] = part
    columns = array((half, width, BLOCK))
    prepared = call(
        prepare_kernel,
        [
            array((half, BLOCK, width)),
            columns,
            columns,
            array(columns.shape, F32),
            array((BLOCK, BLOCK)),
            array((1, BLOCK), F32),
        ],
        "prepare",
        limit=24,
    )(info, lengths, own, kv_other, q_own, q_other)
    parts, prepared = lax.optimization_barrier((parts, prepared))
    total = call(totals_kernel, states, "ctx_totals")(info, lengths, *parts)
    places = lax.axis_size("ctx")
    slices = lax.all_to_all(total.reshape(places, -1, width), "ctx", 0, 0, tiled=True)
    entries = call(entries_kernel, array(slices.shape), "entries")(info, lengths, slices)
    entry = lax.all_to_all(entries, "ctx", 0, 0, tiled=True).reshape(states.shape)
    near = (1, 3, 0)
    made = call(functools.partial(states_kernel, near), [states] * 3, "block_states")(
        info, lengths, *parts, entry
    )
    before = {shift: along_x(part, shift) if shift else part for shift, part in zip(near, made)}

    results = []
    for shifts in GROUPS:
        count = len(shifts) * PER
        vectors = pltpu.VMEM((count, width, BLOCK), F32)
        result = array((count, rows, width))
        mine, others = call(
            functools.partial(solve_kernel, shifts),
            [result, result],
            "solve",
            [
                pltpu.VMEM((count, width, BLOCK + width), BF),
                pltpu.VMEM((width, BLOCK), BF),
                vectors,
                vectors,
                vectors,
                vectors,
                pltpu.VMEM((count, 1, BLOCK), F32),
            ],
            flops=10**9 * count,
            limit=28,
        )(info, reg, *prepared, *(before[s] for s in shifts))
        if shifts == (0,):
            entry, mine = lax.optimization_barrier((entry, mine))
            (part,) = call(functools.partial(states_kernel, (2,)), [states], "block_states")(
                info, lengths, *parts, entry
            )
            before[2] = along_x(part, 2)
        results += [mine, swap(others)]
    return call(
        unpack_kernel,
        array((rows, heads, width)),
        "unpack",
        [pltpu.VMEM((rows * half, width), F32)],
        scalars=1,
    )(info, *results)


def solution(mesh):
    in_specs = (P(("ctx", "head"), None, None, None), P(), P())
    out_specs = P(("ctx", "head"), None, None)
    return jax.shard_map(body, mesh=mesh, in_specs=in_specs, out_specs=out_specs, check_vma=False)
```

```python
import functools
import math

import jax
import jax.numpy as jnp
from jax import lax
from jax.experimental import pallas as pl
from jax.experimental.pallas import tpu as pltpu
from jax.sharding import PartitionSpec as P


ITERS = 10
UNROLL = 5
GROUPS = ((0,), (1, 3), (2,))
BLOCK = 256
HD = 128
NX = 4
NZ = 8
PER = 4
F32 = jnp.float32
BF = jnp.bfloat16
VMEM = pl.BlockSpec(memory_space=pltpu.VMEM)
SMEM = pl.BlockSpec(memory_space=pltpu.SMEM)


def dot(a, b):
    return lax.dot_general(a, b, (((1,), (0,)), ((), ())), preferred_element_type=F32)


def call(kernel, outs, scratch=(), scalars=2, flops=0, limit=16):
    def run(*args):
        return pl.pallas_call(
            kernel,
            in_specs=[SMEM] * scalars + [VMEM] * (len(args) - scalars),
            out_specs=jax.tree.map(lambda _: VMEM, outs),
            out_shape=outs,
            scratch_shapes=list(scratch),
            cost_estimate=pl.CostEstimate(flops=flops, bytes_accessed=1 << 10, transcendentals=0),
            compiler_params=pltpu.CompilerParams(vmem_limit_bytes=limit << 20),
        )(*args)

    return run


def spot(info):
    return info[0] // 2, info[0] % 2, info[1] // NZ, info[1] % NZ


def doc_of(lengths, place):
    doc = jnp.zeros_like(place)
    start = jnp.int32(0)
    for j in range(lengths.shape[0]):
        doc = doc + (place >= start).astype(jnp.int32)
        start = start + lengths[j]
    return doc


def places_of(info, axis):
    x, core, _, _ = spot(info)
    shape = (1, BLOCK) if axis == 1 else (BLOCK, 1)
    entry = lax.broadcasted_iota(jnp.int32, shape, axis)
    half = BLOCK // 2
    base = (info[1] * NX + x) * BLOCK
    return base + jnp.where(entry < half, entry + core * half, entry - core * half)


def diagonals():
    row = lax.broadcasted_iota(jnp.int32, (HD, HD), 0)
    lane = lax.broadcasted_iota(jnp.int32, (HD, HD), 1)
    return row == lane, lane == lax.rem(row + 1, HD)


def rounded(state):
    eye, beside = diagonals()
    whole = state + pltpu.roll(state, HD - 1, 1)
    rest = whole - whole.astype(BF).astype(F32)
    return jnp.where(eye, whole, jnp.where(beside, pltpu.roll(rest, 1, 1), state)).astype(BF)


def started(state):
    _, beside = diagonals()
    return jnp.where(beside, 0.0, state)


def pack_kernel(keys_first, info, x_ref, out_ref, stage):
    rows, count, _ = x_ref.shape
    part = x_ref[...].astype(F32)
    stage[...] = part.reshape(rows * count, HD)
    if keys_first:

        @pl.when(pl.program_id(0) == 0)
        def _():
            scale = lax.rsqrt(jnp.mean(part * part, axis=-1, keepdims=True) + 1e-06)
            stage[...] = (part * scale / math.sqrt(HD)).reshape(rows * count, HD)

    for h in range(count):
        out_ref[0, h] = stage[pl.ds(h, rows, stride=count), :].astype(BF)


def pack(info, qkv, kinds, count, other, far=False):
    rows = qkv.shape[0]

    def place(g, info):
        core = info[0] % 2
        core = 1 - core if other else core
        if count == 16:
            return 0, 2 * kinds[0] + core, 0
        pair = info[0] // 4
        pair = 1 - pair if far else pair
        return 0, 4 * (kinds[0] + g) + 2 * core + pair, 0

    return pl.pallas_call(
        functools.partial(pack_kernel, kinds[0] == 1),
        grid_spec=pltpu.PrefetchScalarGridSpec(
            num_scalar_prefetch=1,
            grid=(len(kinds),),
            in_specs=[pl.BlockSpec((rows, count, HD), place)],
            out_specs=pl.BlockSpec((1, count, rows, HD), lambda g, info: (g, 0, 0, 0)),
            scratch_shapes=[pltpu.VMEM((rows * count, HD), F32)],
        ),
        out_shape=jax.ShapeDtypeStruct((len(kinds), count, rows, HD), BF),
        compiler_params=pltpu.CompilerParams(vmem_limit_bytes=12 << 20),
        cost_estimate=pl.CostEstimate(flops=0, bytes_accessed=1 << 10, transcendentals=0),
        name="pack",
    )(info, qkv)


def sums_kernel(shift, info, lengths, own, other, out):
    x, _, _, _ = spot(info)
    place = places_of(info, 1)
    last = (info[1] * NX + x + 1) * BLOCK - 1
    tail = (doc_of(lengths, place) == doc_of(lengths, last)).astype(F32).astype(BF)
    for j in range(PER):
        h = ((x ^ shift) % 2) * PER + j
        k = jnp.concatenate([own[0, h], other[0, h]], axis=0)
        v = jnp.concatenate([own[1, h], other[1, h]], axis=0)
        out[j, 0] = rounded(started(dot(k.T * tail, k)))
        out[j, 1] = dot(v.T * tail, k).astype(BF)


def weighted(out, terms):
    for j in range(PER):
        for which in range(2):
            total = jnp.zeros((HD, HD), F32)
            for weight, part in terms:
                total = total + weight * part[j, which].astype(F32)
            out[j, which] = rounded(total) if which == 0 else total.astype(BF)


def block_docs(info, lengths):
    first = info[1] * NX * BLOCK
    return [doc_of(lengths, first + b * BLOCK - 1) for b in range(NX + 1)]


def pick(values, place):
    out = values[0]
    for i in range(1, len(values)):
        out = jnp.where(place == i, values[i], out)
    return out


def totals_kernel(info, lengths, p0, p1, p2, p3, out):
    x, _, _, _ = spot(info)
    docs = block_docs(info, lengths)
    terms = []
    for shift, part in enumerate((p0, p1, p2, p3)):
        doc = pick(docs[1:], (x ^ shift))
        terms.append(((doc == docs[NX]).astype(F32), part))
    weighted(out, terms)


def entries_kernel(info, lengths, parts, out):
    count, rows, _ = parts.shape
    width = NX * BLOCK
    docs = [doc_of(lengths, c * width - 1) for c in range(count + 1)]
    per = HD // rows
    symmetric = (info[1] // per) % 2 == 0
    row = (info[1] % per) * rows + lax.broadcasted_iota(jnp.int32, (rows, HD), 0)
    lane = lax.broadcasted_iota(jnp.int32, (rows, HD), 1)
    eye = (row == lane) & symmetric
    beside = (lane == lax.rem(row + 1, HD)) & symmetric
    running = jnp.zeros((rows, HD), F32)
    for c in range(count):
        whole = running + pltpu.roll(running, HD - 1, 1)
        rest = pltpu.roll(whole - whole.astype(BF).astype(F32), 1, 1)
        out[c] = jnp.where(eye, whole, jnp.where(beside, rest, running)).astype(BF)
        same = (docs[c + 1] == docs[c]).astype(F32)
        running = same * running + parts[c].astype(F32)


def states_kernel(shifts, info, lengths, p0, p1, p2, p3, entry, *outs):
    x, _, _, _ = spot(info)
    docs = block_docs(info, lengths)
    weights = []
    for shift in shifts:
        mine = x ^ shift
        wanted = pick(docs[:NX], mine)
        row = [(docs[0] == wanted).astype(F32)]
        for back in range(NX):
            b = x ^ back
            row.append(((b < mine) & (pick(docs[1:], b) == wanted)).astype(F32))
        weights.append(row)
    for j in range(PER):
        for which in range(2):
            parts = [part[j, which].astype(F32) for part in (entry, p0, p1, p2, p3)]
            for row, out in zip(weights, outs):
                total = row[0] * parts[0]
                for weight, part in zip(row[1:], parts[1:]):
                    total = total + weight * part
                out[j, which] = rounded(total) if which == 0 else total.astype(BF)


def prepare_kernel(
    info, lengths, far_own, far_other, near_own, near_other, q_own, q_other,
    keys, key_t, value_t, query, same, valid,
):
    x, _, _, _ = spot(info)
    before = doc_of(lengths, (info[1] * NX + x) * BLOCK - 1)
    lane = places_of(info, 1)
    row = places_of(info, 0)
    lane_doc = doc_of(lengths, lane)
    valid[...] = (lane_doc == before).astype(F32)
    same[...] = ((doc_of(lengths, row) == lane_doc) & (row <= lane)).astype(F32).astype(BF)

    for far in range(2):
        own, other = ((near_own, near_other), (far_own, far_other))[far]
        base = 2 * PER * ((x // 2) ^ far)

        def one(pair, carried):
            for i in (2 * pair, 2 * pair + 1):
                h = base + i
                k = jnp.concatenate([own[0, i], other[0, i]], axis=0)
                keys[h] = k
                key_t[h] = k.T
                value_t[h] = jnp.concatenate([own[1, i], other[1, i]], axis=0).T
                q = jnp.concatenate([q_own[0, h], q_other[0, h]], axis=0).T.astype(F32)
                scale = lax.rsqrt(jnp.mean(q * q, axis=0, keepdims=True) + 1e-06)
                query[h] = q * scale / math.sqrt(HD)
            return carried

        lax.fori_loop(0, PER, one, 0)


def solve_kernel(shifts, info, reg, keys, key_t, value_t, query, same, valid, *rest):
    states, rest = rest[: len(shifts)], rest[len(shifts) :]
    out_own, out_other, lhs, held_valid, diagonal, direction, residual, solution, norm = rest
    x, core, _, _ = spot(info)
    held_valid[...] = jnp.broadcast_to(valid[...], (HD, BLOCK)).astype(BF)
    eye, beside = diagonals()
    count = len(shifts) * PER
    unroll = UNROLL if count > PER else ITERS
    head = [(x ^ shifts[i // PER]) * PER + i % PER for i in range(count)]

    def state(i, which):
        return states[i // PER][i % PER, which]

    for i in range(count):
        held = state(i, 0).astype(F32)
        plain = jnp.where(eye, 0.0, jnp.where(beside, held.T, held)).astype(BF)
        lhs[i, :, 0:BLOCK] = key_t[head[i]]
        lhs[i, :, BLOCK:] = plain
        middle = jnp.sum(jnp.where(eye | beside, held, 0.0), axis=1, keepdims=True)
        diagonal[i] = middle * valid[...] + reg[core * 16 + head[i]]
        q = query[head[i]]
        direction[i] = q
        residual[i] = q
        solution[i] = jnp.zeros_like(q)
        norm[i] = jnp.sum(q * q, axis=0, keepdims=True)

    def scores(i, rounded_vector):
        return dot(keys[head[i]], rounded_vector).astype(BF) * same[...]

    def apply(i):
        p = direction[i].astype(BF)
        return jnp.concatenate([scores(i, p), p * held_valid[...]], axis=0)

    def update(i, applied):
        product = dot(lhs[i], applied)
        for c in (slice(0, BLOCK // 2), slice(BLOCK // 2, BLOCK)):
            p = direction[i, :, c]
            image = product[:, c] + diagonal[i, :, c] * p
            old = norm[i, :, c]
            step = old / (jnp.sum(p * image, axis=0, keepdims=True) + 1e-06)
            solution[i, :, c] = solution[i, :, c] + step * p
            r = residual[i, :, c] - step * image
            residual[i, :, c] = r
            new = jnp.sum(r * r, axis=0, keepdims=True)
            direction[i, :, c] = r + (new / (old + 1e-06)) * p
            norm[i, :, c] = new

    def staggered(first, second, total, lag):
        held = {}
        for t in range(total + lag):
            if t < total:
                held[t] = first(t % count)
            if t >= lag:
                second((t - lag) % count, held.pop(t - lag))

    def iterate(_, carried):
        staggered(apply, update, unroll * count, 3 if count > PER else 2)
        return carried

    def apply_last(i):
        u = solution[i]
        high = u.astype(BF)
        low = (u - high.astype(F32)).astype(BF)
        return jnp.concatenate(
            [scores(i, high), high * held_valid[...], low * held_valid[...]], axis=0
        )

    def finish(i, applied):
        values = state(i, 1)
        whole = jnp.concatenate([value_t[head[i]], values, values], axis=1)
        result = dot(whole, applied).T.astype(BF)
        out_own[i] = result[0 : BLOCK // 2]
        out_other[i] = result[BLOCK // 2 :]

    lax.fori_loop(0, ITERS // unroll, iterate, 0)
    staggered(apply_last, finish, count, 2)


def unpack_kernel(info, *rest):
    parts, (out_ref, stage) = rest[:-2], rest[-2:]
    x, core, _, _ = spot(info)
    rows = out_ref.shape[0]
    for other in range(2):
        for g, shifts in enumerate(GROUPS):
            part = parts[2 * g + other]
            for i in range(len(shifts) * PER):
                h = (x ^ shifts[i // PER]) * PER + i % PER
                stage[pl.ds(h, rows, stride=16), :] = part[i].astype(F32)
        half = core if other == 0 else 1 - core
        first = pl.multiple_of(half * 16, 16)
        out_ref[:, pl.ds(first, 16), :] = stage[...].reshape(rows, 16, HD).astype(BF)


def body(qkv, lengths, reg):
    rows, _, heads, width = qkv.shape
    half = heads // 2
    index = jnp.arange(2, dtype=jnp.int32)
    info = jnp.where(index == 0, lax.axis_index("head"), lax.axis_index("ctx")).astype(jnp.int32)

    def array(shape, dtype=BF):
        return jax.ShapeDtypeStruct(shape, dtype)

    def swap(a):
        return lax.ppermute(a, "head", [(i, i ^ 1) for i in range(2 * NX)])

    def along_x(a, shift):
        return lax.ppermute(
            a, "head", [(i, 2 * ((i // 2) ^ shift) + i % 2) for i in range(2 * NX)]
        )

    def relay(a):
        ring = [(2 * x, 2 * ((x + 1) % NX)) for x in range(NX)]
        back = [(2 * x + 1, 2 * ((x - 1) % NX) + 1) for x in range(NX)]
        return lax.ppermute(a, "head", ring + back)

    def after(a, *others):
        return lax.optimization_barrier((a, *others))[0]

    flat = qkv.reshape(rows, 3 * heads, width)
    first = pltpu.with_memory_space_constraint(flat, pltpu.HBM)
    key_value, query = (1, 2), (0,)
    far_send = pack(info, first, key_value, 8, True, True)
    far_other = swap(far_send)
    far_own = pack(after(info, far_send), flat, key_value, 8, False, True)
    near_send = pack(after(info, far_own), flat, key_value, 8, True)
    near_other = swap(near_send)

    states = array((PER, 2, width, width))

    def sums(shift, own, other):
        return call(functools.partial(sums_kernel, shift), states)(info, lengths, own, other)

    parts = [None] * NX
    hop = sums(2, after(far_own, near_send), far_other)
    parts[2] = relay(hop)
    third = sums(3, after(far_own, hop), far_other)
    parts[3] = along_x(third, 3)
    near_own = pack(after(info, third), flat, key_value, 8, False)
    second = sums(1, near_own, near_other)
    parts[1] = along_x(second, 1)
    parts[2] = relay(parts[2])
    late = after(info, second)
    q_send = pack(late, flat, query, 16, True)
    q_other = swap(q_send)
    q_own = pack(after(info, q_send), flat, query, 16, False)
    parts[0] = sums(0, after(near_own, second), near_other)
    columns = array((half, width, BLOCK))
    prepared = call(
        prepare_kernel,
        [
            array((half, BLOCK, width)),
            columns,
            columns,
            array(columns.shape, F32),
            array((BLOCK, BLOCK)),
            array((1, BLOCK), F32),
        ],
        limit=24,
    )(info, lengths, far_own, far_other, near_own, near_other, q_own, q_other)
    parts, prepared = lax.optimization_barrier((parts, prepared))
    total = call(totals_kernel, states)(info, lengths, *parts)
    places = lax.axis_size("ctx")
    slices = lax.all_to_all(total.reshape(places, -1, width), "ctx", 0, 0, tiled=True)
    entries = call(entries_kernel, array(slices.shape))(info, lengths, slices)
    entry = lax.all_to_all(entries, "ctx", 0, 0, tiled=True).reshape(states.shape)
    near = (1, 3, 0)
    made = call(functools.partial(states_kernel, near), [states] * 3)(info, lengths, *parts, entry)
    before = {shift: along_x(part, shift) if shift else part for shift, part in zip(near, made)}

    results = []
    for shifts in GROUPS:
        count = len(shifts) * PER
        vectors = pltpu.VMEM((count, width, BLOCK), F32)
        result = array((count, rows, width))
        mine, others = call(
            functools.partial(solve_kernel, shifts),
            [result, result],
            [
                pltpu.VMEM((count, width, BLOCK + width), BF),
                pltpu.VMEM((width, BLOCK), BF),
                vectors,
                vectors,
                vectors,
                vectors,
                pltpu.VMEM((count, 1, BLOCK), F32),
            ],
            flops=10**9 * count,
            limit=28,
        )(info, reg, *prepared, *(before[s] for s in shifts))
        if shifts == (0,):
            entry, mine = lax.optimization_barrier((entry, mine))
            (part,) = call(functools.partial(states_kernel, (2,)), [states])(
                info, lengths, *parts, entry
            )
            before[2] = along_x(part, 2)
        results += [mine, swap(others)]
    return call(
        unpack_kernel,
        array((rows, heads, width)),
        [pltpu.VMEM((rows * half, width), F32)],
        scalars=1,
    )(info, *results)


def solution(mesh):
    in_specs = (P(("ctx", "head"), None, None, None), P(), P())
    out_specs = P(("ctx", "head"), None, None)

    return jax.shard_map(body, mesh=mesh, in_specs=in_specs, out_specs=out_specs, check_vma=False)
```

```python
import functools
import math

import jax
import jax.numpy as jnp
from jax import lax
from jax.experimental import pallas as pl
from jax.experimental.pallas import tpu as pltpu
from jax.sharding import PartitionSpec as P


ITERS = 10
UNROLL = 5
GROUPS = ((0,), (1, 3), (2,))
BLOCK = 256
HD = 128
NX = 4
NZ = 8
PER = 4
F32 = jnp.float32
BF = jnp.bfloat16
VMEM = pl.BlockSpec(memory_space=pltpu.VMEM)
SMEM = pl.BlockSpec(memory_space=pltpu.SMEM)


def dot(a, b):
    return lax.dot_general(a, b, (((1,), (0,)), ((), ())), preferred_element_type=F32)


def call(kernel, outs, scratch=(), scalars=2, flops=0, limit=16):
    def run(*args):
        return pl.pallas_call(
            kernel,
            in_specs=[SMEM] * scalars + [VMEM] * (len(args) - scalars),
            out_specs=jax.tree.map(lambda _: VMEM, outs),
            out_shape=outs,
            scratch_shapes=list(scratch),
            cost_estimate=pl.CostEstimate(flops=flops, bytes_accessed=1 << 10, transcendentals=0),
            compiler_params=pltpu.CompilerParams(vmem_limit_bytes=limit << 20),
        )(*args)

    return run


def spot(info):
    return info[0] // 2, info[0] % 2, info[1] // NZ, info[1] % NZ


def doc_of(lengths, place):
    doc = jnp.zeros_like(place)
    start = jnp.int32(0)
    for j in range(lengths.shape[0]):
        doc = doc + (place >= start).astype(jnp.int32)
        start = start + lengths[j]
    return doc


def places_of(info, axis):
    x, core, _, _ = spot(info)
    shape = (1, BLOCK) if axis == 1 else (BLOCK, 1)
    entry = lax.broadcasted_iota(jnp.int32, shape, axis)
    half = BLOCK // 2
    base = (info[1] * NX + x) * BLOCK
    return base + jnp.where(entry < half, entry + core * half, entry - core * half)


def diagonals():
    row = lax.broadcasted_iota(jnp.int32, (HD, HD), 0)
    lane = lax.broadcasted_iota(jnp.int32, (HD, HD), 1)
    return row == lane, lane == lax.rem(row + 1, HD)


def rounded(state):
    eye, beside = diagonals()
    whole = state + pltpu.roll(state, HD - 1, 1)
    rest = whole - whole.astype(BF).astype(F32)
    return jnp.where(eye, whole, jnp.where(beside, pltpu.roll(rest, 1, 1), state)).astype(BF)


def started(state):
    _, beside = diagonals()
    return jnp.where(beside, 0.0, state)


def pack_kernel(keys_first, info, x_ref, out_ref, stage):
    rows, count, _ = x_ref.shape
    part = x_ref[...].astype(F32)
    stage[...] = part.reshape(rows * count, HD)
    if keys_first:

        @pl.when(pl.program_id(0) == 0)
        def _():
            scale = lax.rsqrt(jnp.mean(part * part, axis=-1, keepdims=True) + 1e-06)
            stage[...] = (part * scale / math.sqrt(HD)).reshape(rows * count, HD)

    for h in range(count):
        out_ref[0, h] = stage[pl.ds(h, rows, stride=count), :].astype(BF)


def pack(info, qkv, kinds, count, other, far=False):
    rows = qkv.shape[0]

    def place(g, info):
        core = info[0] % 2
        core = 1 - core if other else core
        if count == 16:
            return 0, 2 * kinds[0] + core, 0
        pair = info[0] // 4
        pair = 1 - pair if far else pair
        return 0, 4 * (kinds[0] + g) + 2 * core + pair, 0

    return pl.pallas_call(
        functools.partial(pack_kernel, kinds[0] == 1),
        grid_spec=pltpu.PrefetchScalarGridSpec(
            num_scalar_prefetch=1,
            grid=(len(kinds),),
            in_specs=[pl.BlockSpec((rows, count, HD), place)],
            out_specs=pl.BlockSpec((1, count, rows, HD), lambda g, info: (g, 0, 0, 0)),
            scratch_shapes=[pltpu.VMEM((rows * count, HD), F32)],
        ),
        out_shape=jax.ShapeDtypeStruct((len(kinds), count, rows, HD), BF),
        compiler_params=pltpu.CompilerParams(vmem_limit_bytes=12 << 20),
        cost_estimate=pl.CostEstimate(flops=0, bytes_accessed=1 << 10, transcendentals=0),
        name="pack",
    )(info, qkv)


def sums_kernel(shift, info, lengths, own, other, out):
    x, _, _, _ = spot(info)
    place = places_of(info, 1)
    last = (info[1] * NX + x + 1) * BLOCK - 1
    tail = (doc_of(lengths, place) == doc_of(lengths, last)).astype(F32).astype(BF)
    for j in range(PER):
        h = ((x ^ shift) % 2) * PER + j
        k = jnp.concatenate([own[0, h], other[0, h]], axis=0)
        v = jnp.concatenate([own[1, h], other[1, h]], axis=0)
        out[j, 0] = rounded(started(dot(k.T * tail, k)))
        out[j, 1] = dot(v.T * tail, k).astype(BF)


def weighted(out, terms):
    for j in range(PER):
        for which in range(2):
            total = jnp.zeros((HD, HD), F32)
            for weight, part in terms:
                total = total + weight * part[j, which].astype(F32)
            out[j, which] = rounded(total) if which == 0 else total.astype(BF)


def block_docs(info, lengths):
    first = info[1] * NX * BLOCK
    return [doc_of(lengths, first + b * BLOCK - 1) for b in range(NX + 1)]


def pick(values, place):
    out = values[0]
    for i in range(1, len(values)):
        out = jnp.where(place == i, values[i], out)
    return out


def totals_kernel(info, lengths, p0, p1, p2, p3, out):
    x, _, _, _ = spot(info)
    docs = block_docs(info, lengths)
    terms = []
    for shift, part in enumerate((p0, p1, p2, p3)):
        doc = pick(docs[1:], (x ^ shift))
        terms.append(((doc == docs[NX]).astype(F32), part))
    weighted(out, terms)


def entries_kernel(info, lengths, parts, out):
    count, rows, _ = parts.shape
    width = NX * BLOCK
    docs = [doc_of(lengths, c * width - 1) for c in range(count + 1)]
    per = HD // rows
    symmetric = (info[1] // per) % 2 == 0
    row = (info[1] % per) * rows + lax.broadcasted_iota(jnp.int32, (rows, HD), 0)
    lane = lax.broadcasted_iota(jnp.int32, (rows, HD), 1)
    eye = (row == lane) & symmetric
    beside = (lane == lax.rem(row + 1, HD)) & symmetric
    running = jnp.zeros((rows, HD), F32)
    for c in range(count):
        whole = running + pltpu.roll(running, HD - 1, 1)
        rest = pltpu.roll(whole - whole.astype(BF).astype(F32), 1, 1)
        out[c] = jnp.where(eye, whole, jnp.where(beside, rest, running)).astype(BF)
        same = (docs[c + 1] == docs[c]).astype(F32)
        running = same * running + parts[c].astype(F32)


def states_kernel(shifts, info, lengths, p0, p1, p2, p3, entry, *outs):
    x, _, _, _ = spot(info)
    docs = block_docs(info, lengths)
    weights = []
    for shift in shifts:
        mine = x ^ shift
        wanted = pick(docs[:NX], mine)
        row = [(docs[0] == wanted).astype(F32)]
        for back in range(NX):
            b = x ^ back
            row.append(((b < mine) & (pick(docs[1:], b) == wanted)).astype(F32))
        weights.append(row)
    for j in range(PER):
        for which in range(2):
            parts = [part[j, which].astype(F32) for part in (entry, p0, p1, p2, p3)]
            for row, out in zip(weights, outs):
                total = row[0] * parts[0]
                for weight, part in zip(row[1:], parts[1:]):
                    total = total + weight * part
                out[j, which] = rounded(total) if which == 0 else total.astype(BF)


def prepare_kernel(
    info, lengths, far_own, far_other, near_own, near_other, q_own, q_other,
    keys, key_t, value_t, query, same, valid,
):
    x, _, _, _ = spot(info)
    before = doc_of(lengths, (info[1] * NX + x) * BLOCK - 1)
    lane = places_of(info, 1)
    row = places_of(info, 0)
    lane_doc = doc_of(lengths, lane)
    valid[...] = (lane_doc == before).astype(F32)
    same[...] = ((doc_of(lengths, row) == lane_doc) & (row <= lane)).astype(F32).astype(BF)

    for far in range(2):
        own, other = ((near_own, near_other), (far_own, far_other))[far]
        base = 2 * PER * ((x // 2) ^ far)

        def one(pair, carried):
            for i in (2 * pair, 2 * pair + 1):
                h = base + i
                k = jnp.concatenate([own[0, i], other[0, i]], axis=0)
                keys[h] = k
                key_t[h] = k.T
                value_t[h] = jnp.concatenate([own[1, i], other[1, i]], axis=0).T
                q = jnp.concatenate([q_own[0, h], q_other[0, h]], axis=0).T.astype(F32)
                scale = lax.rsqrt(jnp.mean(q * q, axis=0, keepdims=True) + 1e-06)
                query[h] = q * scale / math.sqrt(HD)
            return carried

        lax.fori_loop(0, PER, one, 0)


def solve_kernel(shifts, info, reg, keys, key_t, value_t, query, same, valid, *rest):
    states, rest = rest[: len(shifts)], rest[len(shifts) :]
    out_own, out_other, lhs, held_valid, diagonal, direction, residual, solution, norm = rest
    x, core, _, _ = spot(info)
    held_valid[...] = jnp.broadcast_to(valid[...], (HD, BLOCK)).astype(BF)
    eye, beside = diagonals()
    count = len(shifts) * PER
    unroll = UNROLL if count > PER else ITERS
    head = [(x ^ shifts[i // PER]) * PER + i % PER for i in range(count)]

    def state(i, which):
        return states[i // PER][i % PER, which]

    for i in range(count):
        held = state(i, 0).astype(F32)
        plain = jnp.where(eye, 0.0, jnp.where(beside, held.T, held)).astype(BF)
        lhs[i, :, 0:BLOCK] = key_t[head[i]]
        lhs[i, :, BLOCK:] = plain
        middle = jnp.sum(jnp.where(eye | beside, held, 0.0), axis=1, keepdims=True)
        diagonal[i] = middle * valid[...] + reg[core * 16 + head[i]]
        q = query[head[i]]
        direction[i] = q
        residual[i] = q
        solution[i] = jnp.zeros_like(q)
        norm[i] = jnp.sum(q * q, axis=0, keepdims=True)

    def scores(i, rounded_vector):
        return dot(keys[head[i]], rounded_vector).astype(BF) * same[...]

    def apply(i):
        p = direction[i].astype(BF)
        return jnp.concatenate([scores(i, p), p * held_valid[...]], axis=0)

    def update(i, applied):
        product = dot(lhs[i], applied)
        for c in (slice(0, BLOCK // 2), slice(BLOCK // 2, BLOCK)):
            p = direction[i, :, c]
            image = product[:, c] + diagonal[i, :, c] * p
            old = norm[i, :, c]
            step = old / (jnp.sum(p * image, axis=0, keepdims=True) + 1e-06)
            solution[i, :, c] = solution[i, :, c] + step * p
            r = residual[i, :, c] - step * image
            residual[i, :, c] = r
            new = jnp.sum(r * r, axis=0, keepdims=True)
            direction[i, :, c] = r + (new / (old + 1e-06)) * p
            norm[i, :, c] = new

    def staggered(first, second, total, lag):
        held = {}
        for t in range(total + lag):
            if t < total:
                held[t] = first(t % count)
            if t >= lag:
                second((t - lag) % count, held.pop(t - lag))

    def iterate(_, carried):
        staggered(apply, update, unroll * count, 3 if count > PER else 2)
        return carried

    def apply_last(i):
        u = solution[i]
        high = u.astype(BF)
        low = (u - high.astype(F32)).astype(BF)
        return jnp.concatenate(
            [scores(i, high), high * held_valid[...], low * held_valid[...]], axis=0
        )

    def finish(i, applied):
        values = state(i, 1)
        whole = jnp.concatenate([value_t[head[i]], values, values], axis=1)
        result = dot(whole, applied).T.astype(BF)
        out_own[i] = result[0 : BLOCK // 2]
        out_other[i] = result[BLOCK // 2 :]

    lax.fori_loop(0, ITERS // unroll, iterate, 0)
    staggered(apply_last, finish, count, 2)


def unpack_kernel(info, *rest):
    x, _, _, _ = spot(info)
    parts, (out_ref, stage) = rest[: len(GROUPS)], rest[-2:]
    rows = out_ref.shape[0]
    for shifts, part in zip(GROUPS, parts):
        for i in range(len(shifts) * PER):
            h = (x ^ shifts[i // PER]) * PER + i % PER
            stage[pl.ds(h, rows, stride=16), :] = part[i].astype(F32)
    out_ref[...] = stage[...].reshape(rows, 16, HD).astype(BF)


def unpack(info, parts, other, shape, base=()):
    rows = shape[0]

    def place(g, info):
        core = info[0] % 2
        return 0, 1 - core if other else core, 0

    return pl.pallas_call(
        unpack_kernel,
        grid_spec=pltpu.PrefetchScalarGridSpec(
            num_scalar_prefetch=1,
            grid=(1,),
            in_specs=[VMEM] * len(parts) + [pl.BlockSpec(memory_space=pl.ANY)] * len(base),
            out_specs=pl.BlockSpec((rows, 16, HD), place),
            scratch_shapes=[pltpu.VMEM((rows * 16, HD), F32)],
        ),
        out_shape=jax.ShapeDtypeStruct(shape, BF),
        input_output_aliases={1 + len(parts): 0} if base else {},
        compiler_params=pltpu.CompilerParams(vmem_limit_bytes=12 << 20),
        name="unpack",
    )(info, *parts, *base)


def body(qkv, lengths, reg):
    rows, _, heads, width = qkv.shape
    half = heads // 2
    index = jnp.arange(2, dtype=jnp.int32)
    info = jnp.where(index == 0, lax.axis_index("head"), lax.axis_index("ctx")).astype(jnp.int32)

    def array(shape, dtype=BF):
        return jax.ShapeDtypeStruct(shape, dtype)

    def swap(a):
        return lax.ppermute(a, "head", [(i, i ^ 1) for i in range(2 * NX)])

    def along_x(a, shift):
        return lax.ppermute(
            a, "head", [(i, 2 * ((i // 2) ^ shift) + i % 2) for i in range(2 * NX)]
        )

    def relay(a):
        ring = [(2 * x, 2 * ((x + 1) % NX)) for x in range(NX)]
        back = [(2 * x + 1, 2 * ((x - 1) % NX) + 1) for x in range(NX)]
        return lax.ppermute(a, "head", ring + back)

    def after(a, *others):
        return lax.optimization_barrier((a, *others))[0]

    flat = qkv.reshape(rows, 3 * heads, width)
    first = pltpu.with_memory_space_constraint(flat, pltpu.HBM)
    key_value, query = (1, 2), (0,)
    far_send = pack(info, first, key_value, 8, True, True)
    far_other = swap(far_send)
    far_own = pack(after(info, far_send), flat, key_value, 8, False, True)
    near_send = pack(after(info, far_own), flat, key_value, 8, True)
    near_other = swap(near_send)

    states = array((PER, 2, width, width))

    def sums(shift, own, other):
        return call(functools.partial(sums_kernel, shift), states)(info, lengths, own, other)

    parts = [None] * NX
    hop = sums(2, after(far_own, near_send), far_other)
    parts[2] = relay(hop)
    third = sums(3, after(far_own, hop), far_other)
    parts[3] = along_x(third, 3)
    near_own = pack(after(info, third), flat, key_value, 8, False)
    second = sums(1, near_own, near_other)
    parts[1] = along_x(second, 1)
    parts[2] = relay(parts[2])
    late = after(info, second)
    q_send = pack(late, flat, query, 16, True)
    q_other = swap(q_send)
    q_own = pack(after(info, q_send), flat, query, 16, False)
    parts[0] = sums(0, after(near_own, second), near_other)
    columns = array((half, width, BLOCK))
    prepared = call(
        prepare_kernel,
        [
            array((half, BLOCK, width)),
            columns,
            columns,
            array(columns.shape, F32),
            array((BLOCK, BLOCK)),
            array((1, BLOCK), F32),
        ],
        limit=24,
    )(info, lengths, far_own, far_other, near_own, near_other, q_own, q_other)
    parts, prepared = lax.optimization_barrier((parts, prepared))
    total = call(totals_kernel, states)(info, lengths, *parts)
    places = lax.axis_size("ctx")
    slices = lax.all_to_all(total.reshape(places, -1, width), "ctx", 0, 0, tiled=True)
    entries = call(entries_kernel, array(slices.shape))(info, lengths, slices)
    entry = lax.all_to_all(entries, "ctx", 0, 0, tiled=True).reshape(states.shape)
    masks = (1, 3, 0, 2)
    made = call(functools.partial(states_kernel, masks), [states] * NX)(
        info, lengths, *parts, entry
    )
    before = dict(zip(masks, made))
    for shift in (1, 3):
        before[shift] = along_x(before[shift], shift)

    mine, theirs = [], []
    for shifts in GROUPS:
        count = len(shifts) * PER
        vectors = pltpu.VMEM((count, width, BLOCK), F32)
        result = array((count, rows, width))
        kept, others = call(
            functools.partial(solve_kernel, shifts),
            [result, result],
            [
                pltpu.VMEM((count, width, BLOCK + width), BF),
                pltpu.VMEM((width, BLOCK), BF),
                vectors,
                vectors,
                vectors,
                vectors,
                pltpu.VMEM((count, 1, BLOCK), F32),
            ],
            flops=10**9 * count,
            limit=28,
        )(info, reg, *prepared, *(before[s] for s in shifts))
        if shifts == (0,):
            before[2] = along_x(after(before[2], kept), 2)
        mine.append(kept)
        theirs.append(swap(others))
    shape = (rows, heads, width)
    out = unpack(info, mine, False, shape)
    return unpack(info, theirs, True, shape, (out,))


def solution(mesh):
    in_specs = (P(("ctx", "head"), None, None, None), P(), P())
    out_specs = P(("ctx", "head"), None, None)

    return jax.shard_map(body, mesh=mesh, in_specs=in_specs, out_specs=out_specs, check_vma=False)
```

```python
import functools
import math

import jax
import jax.numpy as jnp
from jax import lax
from jax.experimental import pallas as pl
from jax.experimental.pallas import tpu as pltpu
from jax.sharding import PartitionSpec as P


ITERS = 10
UNROLL = 5
GROUPS = ((0,), (1, 3), (2,))
BLOCK = 256
HD = 128
NX = 4
NZ = 8
PER = 4
F32 = jnp.float32
BF = jnp.bfloat16
VMEM = pl.BlockSpec(memory_space=pltpu.VMEM)
SMEM = pl.BlockSpec(memory_space=pltpu.SMEM)


def dot(a, b):
    return lax.dot_general(a, b, (((1,), (0,)), ((), ())), preferred_element_type=F32)


def call(kernel, outs, scratch=(), scalars=2, flops=0, limit=16):
    def run(*args):
        return pl.pallas_call(
            kernel,
            in_specs=[SMEM] * scalars + [VMEM] * (len(args) - scalars),
            out_specs=jax.tree.map(lambda _: VMEM, outs),
            out_shape=outs,
            scratch_shapes=list(scratch),
            cost_estimate=pl.CostEstimate(flops=flops, bytes_accessed=1 << 10, transcendentals=0),
            compiler_params=pltpu.CompilerParams(vmem_limit_bytes=limit << 20),
        )(*args)

    return run


def spot(info):
    return info[0] // 2, info[0] % 2, info[1] // NZ, info[1] % NZ


def doc_of(lengths, place):
    doc = jnp.zeros_like(place)
    start = jnp.int32(0)
    for j in range(lengths.shape[0]):
        doc = doc + (place >= start).astype(jnp.int32)
        start = start + lengths[j]
    return doc


def places_of(info, axis):
    x, core, _, _ = spot(info)
    shape = (1, BLOCK) if axis == 1 else (BLOCK, 1)
    entry = lax.broadcasted_iota(jnp.int32, shape, axis)
    half = BLOCK // 2
    base = (info[1] * NX + x) * BLOCK
    return base + jnp.where(entry < half, entry + core * half, entry - core * half)


def diagonals():
    row = lax.broadcasted_iota(jnp.int32, (HD, HD), 0)
    lane = lax.broadcasted_iota(jnp.int32, (HD, HD), 1)
    return row == lane, lane == lax.rem(row + 1, HD)


def rounded(state):
    eye, beside = diagonals()
    whole = state + pltpu.roll(state, HD - 1, 1)
    rest = whole - whole.astype(BF).astype(F32)
    return jnp.where(eye, whole, jnp.where(beside, pltpu.roll(rest, 1, 1), state)).astype(BF)


def started(state):
    _, beside = diagonals()
    return jnp.where(beside, 0.0, state)


def pack_kernel(keys_first, info, x_ref, out_ref, stage):
    rows, count, _ = x_ref.shape
    part = x_ref[...].astype(F32)
    stage[...] = part.reshape(rows * count, HD)
    if keys_first:

        @pl.when(pl.program_id(0) == 0)
        def _():
            scale = lax.rsqrt(jnp.mean(part * part, axis=-1, keepdims=True) + 1e-06)
            stage[...] = (part * scale / math.sqrt(HD)).reshape(rows * count, HD)

    for h in range(count):
        out_ref[0, h] = stage[pl.ds(h, rows, stride=count), :].astype(BF)


def pack(info, qkv, kinds, count, other, far=False):
    rows = qkv.shape[0]

    def place(g, info):
        core = info[0] % 2
        core = 1 - core if other else core
        if count == 16:
            return 0, 2 * kinds[0] + core, 0
        pair = info[0] // 4
        pair = 1 - pair if far else pair
        return 0, 4 * (kinds[0] + g) + 2 * core + pair, 0

    return pl.pallas_call(
        functools.partial(pack_kernel, kinds[0] == 1),
        grid_spec=pltpu.PrefetchScalarGridSpec(
            num_scalar_prefetch=1,
            grid=(len(kinds),),
            in_specs=[pl.BlockSpec((rows, count, HD), place)],
            out_specs=pl.BlockSpec((1, count, rows, HD), lambda g, info: (g, 0, 0, 0)),
            scratch_shapes=[pltpu.VMEM((rows * count, HD), F32)],
        ),
        out_shape=jax.ShapeDtypeStruct((len(kinds), count, rows, HD), BF),
        compiler_params=pltpu.CompilerParams(vmem_limit_bytes=12 << 20),
        cost_estimate=pl.CostEstimate(flops=0, bytes_accessed=1 << 10, transcendentals=0),
        name="pack",
    )(info, qkv)


def sums_kernel(shift, info, lengths, own, other, out):
    x, _, _, _ = spot(info)
    place = places_of(info, 1)
    last = (info[1] * NX + x + 1) * BLOCK - 1
    tail = (doc_of(lengths, place) == doc_of(lengths, last)).astype(F32).astype(BF)
    for j in range(PER):
        h = ((x ^ shift) % 2) * PER + j
        k = jnp.concatenate([own[0, h], other[0, h]], axis=0)
        v = jnp.concatenate([own[1, h], other[1, h]], axis=0)
        out[j, 0] = rounded(started(dot(k.T * tail, k)))
        out[j, 1] = dot(v.T * tail, k).astype(BF)


def weighted(out, terms):
    for j in range(PER):
        for which in range(2):
            total = jnp.zeros((HD, HD), F32)
            for weight, part in terms:
                total = total + weight * part[j, which].astype(F32)
            out[j, which] = rounded(total) if which == 0 else total.astype(BF)


def block_docs(info, lengths):
    first = info[1] * NX * BLOCK
    return [doc_of(lengths, first + b * BLOCK - 1) for b in range(NX + 1)]


def pick(values, place):
    out = values[0]
    for i in range(1, len(values)):
        out = jnp.where(place == i, values[i], out)
    return out


def totals_kernel(info, lengths, p0, p1, p2, p3, out):
    x, _, _, _ = spot(info)
    docs = block_docs(info, lengths)
    terms = []
    for shift, part in enumerate((p0, p1, p2, p3)):
        doc = pick(docs[1:], (x ^ shift))
        terms.append(((doc == docs[NX]).astype(F32), part))
    weighted(out, terms)


def entries_kernel(info, lengths, parts, out):
    count, rows, _ = parts.shape
    width = NX * BLOCK
    docs = [doc_of(lengths, c * width - 1) for c in range(count + 1)]
    per = HD // rows
    symmetric = (info[1] // per) % 2 == 0
    row = (info[1] % per) * rows + lax.broadcasted_iota(jnp.int32, (rows, HD), 0)
    lane = lax.broadcasted_iota(jnp.int32, (rows, HD), 1)
    eye = (row == lane) & symmetric
    beside = (lane == lax.rem(row + 1, HD)) & symmetric
    running = jnp.zeros((rows, HD), F32)
    for c in range(count):
        whole = running + pltpu.roll(running, HD - 1, 1)
        rest = pltpu.roll(whole - whole.astype(BF).astype(F32), 1, 1)
        out[c] = jnp.where(eye, whole, jnp.where(beside, rest, running)).astype(BF)
        same = (docs[c + 1] == docs[c]).astype(F32)
        running = same * running + parts[c].astype(F32)


def states_kernel(shifts, info, lengths, p0, p1, p2, p3, entry, *outs):
    x, _, _, _ = spot(info)
    docs = block_docs(info, lengths)
    weights = []
    for shift in shifts:
        mine = x ^ shift
        wanted = pick(docs[:NX], mine)
        row = [(docs[0] == wanted).astype(F32)]
        for back in range(NX):
            b = x ^ back
            row.append(((b < mine) & (pick(docs[1:], b) == wanted)).astype(F32))
        weights.append(row)
    for j in range(PER):
        for which in range(2):
            parts = [part[j, which].astype(F32) for part in (entry, p0, p1, p2, p3)]
            for row, out in zip(weights, outs):
                total = row[0] * parts[0]
                for weight, part in zip(row[1:], parts[1:]):
                    total = total + weight * part
                out[j, which] = rounded(total) if which == 0 else total.astype(BF)


def prepare_kernel(
    info, lengths, far_own, far_other, near_own, near_other, q_own, q_other,
    keys, key_t, value_t, query, same, valid,
):
    x, _, _, _ = spot(info)
    before = doc_of(lengths, (info[1] * NX + x) * BLOCK - 1)
    lane = places_of(info, 1)
    row = places_of(info, 0)
    lane_doc = doc_of(lengths, lane)
    valid[...] = (lane_doc == before).astype(F32)
    same[...] = ((doc_of(lengths, row) == lane_doc) & (row <= lane)).astype(F32).astype(BF)

    for far in range(2):
        own, other = ((near_own, near_other), (far_own, far_other))[far]
        base = 2 * PER * ((x // 2) ^ far)

        def one(pair, carried):
            for i in (2 * pair, 2 * pair + 1):
                h = base + i
                k = jnp.concatenate([own[0, i], other[0, i]], axis=0)
                keys[h] = k
                key_t[h] = k.T
                value_t[h] = jnp.concatenate([own[1, i], other[1, i]], axis=0).T
                q = jnp.concatenate([q_own[0, h], q_other[0, h]], axis=0).T.astype(F32)
                scale = lax.rsqrt(jnp.mean(q * q, axis=0, keepdims=True) + 1e-06)
                query[h] = q * scale / math.sqrt(HD)
            return carried

        lax.fori_loop(0, PER, one, 0)


def solve_kernel(shifts, info, reg, keys, key_t, value_t, query, same, valid, *rest):
    states, rest = rest[: len(shifts)], rest[len(shifts) :]
    out_own, out_other, lhs, held_valid, diagonal, direction, residual, solution, norm = rest
    x, core, _, _ = spot(info)
    held_valid[...] = jnp.broadcast_to(valid[...], (HD, BLOCK)).astype(BF)
    eye, beside = diagonals()
    count = len(shifts) * PER
    unroll = UNROLL if count > PER else ITERS
    head = [(x ^ shifts[i // PER]) * PER + i % PER for i in range(count)]

    def state(i, which):
        return states[i // PER][i % PER, which]

    for i in range(count):
        held = state(i, 0).astype(F32)
        plain = jnp.where(eye, 0.0, jnp.where(beside, held.T, held)).astype(BF)
        lhs[i, :, 0:BLOCK] = key_t[head[i]]
        lhs[i, :, BLOCK:] = plain
        middle = jnp.sum(jnp.where(eye | beside, held, 0.0), axis=1, keepdims=True)
        diagonal[i] = middle * valid[...] + reg[core * 16 + head[i]]
        q = query[head[i]]
        direction[i] = q
        residual[i] = q
        solution[i] = jnp.zeros_like(q)
        norm[i] = jnp.sum(q * q, axis=0, keepdims=True)

    def scores(i, rounded_vector):
        return dot(keys[head[i]], rounded_vector).astype(BF) * same[...]

    def apply(i):
        p = direction[i].astype(BF)
        return jnp.concatenate([scores(i, p), p * held_valid[...]], axis=0)

    def update(i, applied):
        product = dot(lhs[i], applied)
        for c in (slice(0, BLOCK // 2), slice(BLOCK // 2, BLOCK)):
            p = direction[i, :, c]
            image = product[:, c] + diagonal[i, :, c] * p
            old = norm[i, :, c]
            step = old / (jnp.sum(p * image, axis=0, keepdims=True) + 1e-06)
            solution[i, :, c] = solution[i, :, c] + step * p
            r = residual[i, :, c] - step * image
            residual[i, :, c] = r
            new = jnp.sum(r * r, axis=0, keepdims=True)
            direction[i, :, c] = r + (new / (old + 1e-06)) * p
            norm[i, :, c] = new

    def staggered(first, second, total, lag):
        held = {}
        for t in range(total + lag):
            if t < total:
                held[t] = first(t % count)
            if t >= lag:
                second((t - lag) % count, held.pop(t - lag))

    def iterate(_, carried):
        staggered(apply, update, unroll * count, 3 if count > PER else 2)
        return carried

    def apply_last(i):
        u = solution[i]
        high = u.astype(BF)
        low = (u - high.astype(F32)).astype(BF)
        return jnp.concatenate(
            [scores(i, high), high * held_valid[...], low * held_valid[...]], axis=0
        )

    def finish(i, applied):
        values = state(i, 1)
        whole = jnp.concatenate([value_t[head[i]], values, values], axis=1)
        result = dot(whole, applied).T.astype(BF)
        out_own[i] = result[0 : BLOCK // 2]
        out_other[i] = result[BLOCK // 2 :]

    lax.fori_loop(0, ITERS // unroll, iterate, 0)
    staggered(apply_last, finish, count, 2)


def unpack_kernel(info, *rest):
    x, _, _, _ = spot(info)
    parts, (out_ref, stage) = rest[: len(GROUPS)], rest[-2:]
    rows = out_ref.shape[0]
    for shifts, part in zip(GROUPS, parts):
        for i in range(len(shifts) * PER):
            h = (x ^ shifts[i // PER]) * PER + i % PER
            stage[pl.ds(h, rows, stride=16), :] = part[i].astype(F32)
    out_ref[...] = stage[...].reshape(rows, 16, HD).astype(BF)


def unpack(info, parts, other, shape, base=()):
    rows = shape[0]

    def place(g, info):
        core = info[0] % 2
        return 0, 1 - core if other else core, 0

    return pl.pallas_call(
        unpack_kernel,
        grid_spec=pltpu.PrefetchScalarGridSpec(
            num_scalar_prefetch=1,
            grid=(1,),
            in_specs=[VMEM] * len(parts) + [pl.BlockSpec(memory_space=pl.ANY)] * len(base),
            out_specs=pl.BlockSpec((rows, 16, HD), place),
            scratch_shapes=[pltpu.VMEM((rows * 16, HD), F32)],
        ),
        out_shape=jax.ShapeDtypeStruct(shape, BF),
        input_output_aliases={1 + len(parts): 0} if base else {},
        compiler_params=pltpu.CompilerParams(vmem_limit_bytes=12 << 20),
        name="unpack",
    )(info, *parts, *base)


def body(qkv, lengths, reg):
    rows, _, heads, width = qkv.shape
    half = heads // 2
    index = jnp.arange(2, dtype=jnp.int32)
    info = jnp.where(index == 0, lax.axis_index("head"), lax.axis_index("ctx")).astype(jnp.int32)

    def array(shape, dtype=BF):
        return jax.ShapeDtypeStruct(shape, dtype)

    def swap(a):
        return lax.ppermute(a, "head", [(i, i ^ 1) for i in range(2 * NX)])

    def along_x(a, shift):
        return lax.ppermute(
            a, "head", [(i, 2 * ((i // 2) ^ shift) + i % 2) for i in range(2 * NX)]
        )

    def relay(a):
        ring = [(2 * x, 2 * ((x + 1) % NX)) for x in range(NX)]
        back = [(2 * x + 1, 2 * ((x - 1) % NX) + 1) for x in range(NX)]
        return lax.ppermute(a, "head", ring + back)

    def after(a, *others):
        return lax.optimization_barrier((a, *others))[0]

    flat = qkv.reshape(rows, 3 * heads, width)
    first = pltpu.with_memory_space_constraint(flat, pltpu.HBM)
    key_value, query = (1, 2), (0,)
    far_send = pack(info, first, key_value, 8, True, True)
    far_other = swap(far_send)
    far_own = pack(after(info, far_send), flat, key_value, 8, False, True)
    near_send = pack(after(info, far_own), flat, key_value, 8, True)
    near_other = swap(near_send)

    states = array((PER, 2, width, width))

    def sums(shift, own, other):
        return call(functools.partial(sums_kernel, shift), states)(info, lengths, own, other)

    parts = [None] * NX
    hop = sums(2, after(far_own, near_send), far_other)
    parts[2] = relay(hop)
    third = sums(3, after(far_own, hop), far_other)
    parts[3] = along_x(third, 3)
    near_own = pack(after(info, third), flat, key_value, 8, False)
    second = sums(1, near_own, near_other)
    parts[1] = along_x(second, 1)
    parts[2] = relay(parts[2])
    late = after(info, second)
    q_send = pack(late, flat, query, 16, True)
    q_other = swap(q_send)
    q_own = pack(after(info, q_send), flat, query, 16, False)
    parts[0] = sums(0, after(near_own, second), near_other)
    columns = array((half, width, BLOCK))
    prepared = call(
        prepare_kernel,
        [
            array((half, BLOCK, width)),
            columns,
            columns,
            array(columns.shape, F32),
            array((BLOCK, BLOCK)),
            array((1, BLOCK), F32),
        ],
        limit=24,
    )(info, lengths, far_own, far_other, near_own, near_other, q_own, q_other)
    parts, prepared = lax.optimization_barrier((parts, prepared))
    total = call(totals_kernel, states)(info, lengths, *parts)
    places = lax.axis_size("ctx")
    slices = lax.all_to_all(total.reshape(places, -1, width), "ctx", 0, 0, tiled=True)
    entries = call(entries_kernel, array(slices.shape))(info, lengths, slices)
    entry = lax.all_to_all(entries, "ctx", 0, 0, tiled=True).reshape(states.shape)
    masks = (1, 3, 0, 2)
    made = call(functools.partial(states_kernel, masks), [states] * NX)(
        info, lengths, *parts, entry
    )
    before = dict(zip(masks, made))
    for shift in (1, 3):
        before[shift] = along_x(before[shift], shift)

    mine, theirs = [], []
    for shifts in GROUPS:
        count = len(shifts) * PER
        vectors = pltpu.VMEM((count, width, BLOCK), F32)
        result = array((count, rows, width))
        kept, others = call(
            functools.partial(solve_kernel, shifts),
            [result, result],
            [
                pltpu.VMEM((count, width, BLOCK + width), BF),
                pltpu.VMEM((width, BLOCK), BF),
                vectors,
                vectors,
                vectors,
                vectors,
                pltpu.VMEM((count, 1, BLOCK), F32),
            ],
            flops=10**9 * count,
            limit=28,
        )(info, reg, *prepared, *(before[s] for s in shifts))
        if shifts == (0,):
            before[2] = along_x(after(before[2], kept), 2)
        mine.append(kept)
        theirs.append(others)
    theirs[0] = swap(after(theirs[0], mine[1]))
    theirs[1] = swap(theirs[1])
    theirs[2] = swap(theirs[2])
    shape = (rows, heads, width)
    out = unpack(info, mine, False, shape)
    return unpack(info, theirs, True, shape, (out,))


def solution(mesh):
    in_specs = (P(("ctx", "head"), None, None, None), P(), P())
    out_specs = P(("ctx", "head"), None, None)

    return jax.shard_map(body, mesh=mesh, in_specs=in_specs, out_specs=out_specs, check_vma=False)
```

```python
import functools
import math

import jax
import jax.numpy as jnp
from jax import lax
from jax.experimental import pallas as pl
from jax.experimental.pallas import tpu as pltpu
from jax.sharding import PartitionSpec as P


ITERS = 10
UNROLL = 5
GROUPS = ((0,), (1, 3), (2,))
BLOCK = 256
HD = 128
NX = 4
NZ = 8
PER = 4
F32 = jnp.float32
BF = jnp.bfloat16
VMEM = pl.BlockSpec(memory_space=pltpu.VMEM)
SMEM = pl.BlockSpec(memory_space=pltpu.SMEM)


def dot(a, b):
    return lax.dot_general(a, b, (((1,), (0,)), ((), ())), preferred_element_type=F32)


def call(kernel, outs, scratch=(), scalars=2, flops=0, limit=16):
    def run(*args):
        return pl.pallas_call(
            kernel,
            in_specs=[SMEM] * scalars + [VMEM] * (len(args) - scalars),
            out_specs=jax.tree.map(lambda _: VMEM, outs),
            out_shape=outs,
            scratch_shapes=list(scratch),
            cost_estimate=pl.CostEstimate(flops=flops, bytes_accessed=1 << 10, transcendentals=0),
            compiler_params=pltpu.CompilerParams(vmem_limit_bytes=limit << 20),
        )(*args)

    return run


def spot(info):
    return info[0] // 2, info[0] % 2, info[1] // NZ, info[1] % NZ


def doc_of(lengths, place):
    doc = jnp.zeros_like(place)
    start = jnp.int32(0)
    for j in range(lengths.shape[0]):
        doc = doc + (place >= start).astype(jnp.int32)
        start = start + lengths[j]
    return doc


def places_of(info, axis):
    x, core, _, _ = spot(info)
    shape = (1, BLOCK) if axis == 1 else (BLOCK, 1)
    entry = lax.broadcasted_iota(jnp.int32, shape, axis)
    half = BLOCK // 2
    base = (info[1] * NX + x) * BLOCK
    return base + jnp.where(entry < half, entry + core * half, entry - core * half)


def diagonals():
    row = lax.broadcasted_iota(jnp.int32, (HD, HD), 0)
    lane = lax.broadcasted_iota(jnp.int32, (HD, HD), 1)
    return row == lane, lane == lax.rem(row + 1, HD)


def rounded(state):
    eye, beside = diagonals()
    whole = state + pltpu.roll(state, HD - 1, 1)
    rest = whole - whole.astype(BF).astype(F32)
    return jnp.where(eye, whole, jnp.where(beside, pltpu.roll(rest, 1, 1), state)).astype(BF)


def started(state):
    _, beside = diagonals()
    return jnp.where(beside, 0.0, state)


def pack_kernel(keys_first, info, x_ref, out_ref):
    if not keys_first:
        out_ref[0] = jnp.swapaxes(x_ref[...], 0, 1)
        return

    @pl.when(pl.program_id(0) == 0)
    def _():
        part = x_ref[...].astype(F32)
        scale = lax.rsqrt(jnp.mean(part * part, axis=-1, keepdims=True) + 1e-06)
        out_ref[0] = jnp.swapaxes((part * scale / math.sqrt(HD)).astype(BF), 0, 1)

    @pl.when(pl.program_id(0) > 0)
    def _():
        out_ref[0] = jnp.swapaxes(x_ref[...], 0, 1)


def pack(info, qkv, kinds, count, other, far=False):
    rows = qkv.shape[0]

    def place(g, info):
        core = info[0] % 2
        core = 1 - core if other else core
        if count == 16:
            return 0, 2 * kinds[0] + core, 0
        pair = info[0] // 4
        pair = 1 - pair if far else pair
        return 0, 4 * (kinds[0] + g) + 2 * core + pair, 0

    return pl.pallas_call(
        functools.partial(pack_kernel, kinds[0] == 1),
        grid_spec=pltpu.PrefetchScalarGridSpec(
            num_scalar_prefetch=1,
            grid=(len(kinds),),
            in_specs=[pl.BlockSpec((rows, count, HD), place)],
            out_specs=pl.BlockSpec((1, count, rows, HD), lambda g, info: (g, 0, 0, 0)),
        ),
        out_shape=jax.ShapeDtypeStruct((len(kinds), count, rows, HD), BF),
        compiler_params=pltpu.CompilerParams(vmem_limit_bytes=12 << 20),
        cost_estimate=pl.CostEstimate(flops=0, bytes_accessed=1 << 10, transcendentals=0),
        name="pack",
    )(info, qkv)


def sums_kernel(shift, info, lengths, own, other, out):
    x, _, _, _ = spot(info)
    place = places_of(info, 1)
    last = (info[1] * NX + x + 1) * BLOCK - 1
    tail = (doc_of(lengths, place) == doc_of(lengths, last)).astype(F32).astype(BF)
    for j in range(PER):
        h = ((x ^ shift) % 2) * PER + j
        k = jnp.concatenate([own[0, h], other[0, h]], axis=0)
        v = jnp.concatenate([own[1, h], other[1, h]], axis=0)
        out[j, 0] = rounded(started(dot(k.T * tail, k)))
        out[j, 1] = dot(v.T * tail, k).astype(BF)


def weighted(out, terms):
    for j in range(PER):
        for which in range(2):
            total = jnp.zeros((HD, HD), F32)
            for weight, part in terms:
                total = total + weight * part[j, which].astype(F32)
            out[j, which] = rounded(total) if which == 0 else total.astype(BF)


def block_docs(info, lengths):
    first = info[1] * NX * BLOCK
    return [doc_of(lengths, first + b * BLOCK - 1) for b in range(NX + 1)]


def pick(values, place):
    out = values[0]
    for i in range(1, len(values)):
        out = jnp.where(place == i, values[i], out)
    return out


def totals_kernel(info, lengths, p0, p1, p2, p3, out):
    x, _, _, _ = spot(info)
    docs = block_docs(info, lengths)
    terms = []
    for shift, part in enumerate((p0, p1, p2, p3)):
        doc = pick(docs[1:], (x ^ shift))
        terms.append(((doc == docs[NX]).astype(F32), part))
    weighted(out, terms)


def entries_kernel(info, lengths, parts, out):
    count, rows, _ = parts.shape
    width = NX * BLOCK
    docs = [doc_of(lengths, c * width - 1) for c in range(count + 1)]
    per = HD // rows
    symmetric = (info[1] // per) % 2 == 0
    row = (info[1] % per) * rows + lax.broadcasted_iota(jnp.int32, (rows, HD), 0)
    lane = lax.broadcasted_iota(jnp.int32, (rows, HD), 1)
    eye = (row == lane) & symmetric
    beside = (lane == lax.rem(row + 1, HD)) & symmetric
    running = jnp.zeros((rows, HD), F32)
    for c in range(count):
        whole = running + pltpu.roll(running, HD - 1, 1)
        rest = pltpu.roll(whole - whole.astype(BF).astype(F32), 1, 1)
        out[c] = jnp.where(eye, whole, jnp.where(beside, rest, running)).astype(BF)
        same = (docs[c + 1] == docs[c]).astype(F32)
        running = same * running + parts[c].astype(F32)


def states_kernel(shifts, info, lengths, p0, p1, p2, p3, entry, *outs):
    x, _, _, _ = spot(info)
    docs = block_docs(info, lengths)
    weights = []
    for shift in shifts:
        mine = x ^ shift
        wanted = pick(docs[:NX], mine)
        row = [(docs[0] == wanted).astype(F32)]
        for back in range(NX):
            b = x ^ back
            row.append(((b < mine) & (pick(docs[1:], b) == wanted)).astype(F32))
        weights.append(row)
    for j in range(PER):
        for which in range(2):
            parts = [part[j, which].astype(F32) for part in (entry, p0, p1, p2, p3)]
            for row, out in zip(weights, outs):
                total = row[0] * parts[0]
                for weight, part in zip(row[1:], parts[1:]):
                    total = total + weight * part
                out[j, which] = rounded(total) if which == 0 else total.astype(BF)


def prepare_kernel(
    info, lengths, far_own, far_other, near_own, near_other, q_own, q_other,
    keys, key_t, value_t, query, same, valid,
):
    x, _, _, _ = spot(info)
    before = doc_of(lengths, (info[1] * NX + x) * BLOCK - 1)
    lane = places_of(info, 1)
    row = places_of(info, 0)
    lane_doc = doc_of(lengths, lane)
    valid[...] = (lane_doc == before).astype(F32)
    same[...] = ((doc_of(lengths, row) == lane_doc) & (row <= lane)).astype(F32).astype(BF)

    for far in range(2):
        own, other = ((near_own, near_other), (far_own, far_other))[far]
        base = 2 * PER * ((x // 2) ^ far)

        def one(pair, carried):
            for i in (2 * pair, 2 * pair + 1):
                h = base + i
                k = jnp.concatenate([own[0, i], other[0, i]], axis=0)
                keys[h] = k
                key_t[h] = k.T
                value_t[h] = jnp.concatenate([own[1, i], other[1, i]], axis=0).T
                q = jnp.concatenate([q_own[0, h], q_other[0, h]], axis=0).T.astype(F32)
                scale = lax.rsqrt(jnp.mean(q * q, axis=0, keepdims=True) + 1e-06)
                query[h] = q * scale / math.sqrt(HD)
            return carried

        lax.fori_loop(0, PER, one, 0)


def solve_kernel(shifts, info, reg, keys, key_t, value_t, query, same, valid, *rest):
    states, rest = rest[: len(shifts)], rest[len(shifts) :]
    out_own, out_other, lhs, held_valid, diagonal, direction, residual, solution, norm = rest
    x, core, _, _ = spot(info)
    held_valid[...] = jnp.broadcast_to(valid[...], (HD, BLOCK)).astype(BF)
    eye, beside = diagonals()
    count = len(shifts) * PER
    unroll = UNROLL if count > PER else ITERS
    head = [(x ^ shifts[i // PER]) * PER + i % PER for i in range(count)]

    def state(i, which):
        return states[i // PER][i % PER, which]

    for i in range(count):
        held = state(i, 0).astype(F32)
        plain = jnp.where(eye, 0.0, jnp.where(beside, held.T, held)).astype(BF)
        lhs[i, :, 0:BLOCK] = key_t[head[i]]
        lhs[i, :, BLOCK:] = plain
        middle = jnp.sum(jnp.where(eye | beside, held, 0.0), axis=1, keepdims=True)
        diagonal[i] = middle * valid[...] + reg[core * 16 + head[i]]
        q = query[head[i]]
        direction[i] = q
        residual[i] = q
        solution[i] = jnp.zeros_like(q)
        norm[i] = jnp.sum(q * q, axis=0, keepdims=True)

    def scores(i, rounded_vector):
        return dot(keys[head[i]], rounded_vector).astype(BF) * same[...]

    def apply(i):
        p = direction[i].astype(BF)
        return jnp.concatenate([scores(i, p), p * held_valid[...]], axis=0)

    def update(i, applied):
        product = dot(lhs[i], applied)
        for c in (slice(0, BLOCK // 2), slice(BLOCK // 2, BLOCK)):
            p = direction[i, :, c]
            image = product[:, c] + diagonal[i, :, c] * p
            old = norm[i, :, c]
            step = old / (jnp.sum(p * image, axis=0, keepdims=True) + 1e-06)
            solution[i, :, c] = solution[i, :, c] + step * p
            r = residual[i, :, c] - step * image
            residual[i, :, c] = r
            new = jnp.sum(r * r, axis=0, keepdims=True)
            direction[i, :, c] = r + (new / (old + 1e-06)) * p
            norm[i, :, c] = new

    def staggered(first, second, total, lag):
        held = {}
        for t in range(total + lag):
            if t < total:
                held[t] = first(t % count)
            if t >= lag:
                second((t - lag) % count, held.pop(t - lag))

    def iterate(_, carried):
        staggered(apply, update, unroll * count, 3 if count > PER else 2)
        return carried

    def apply_last(i):
        u = solution[i]
        high = u.astype(BF)
        low = (u - high.astype(F32)).astype(BF)
        return jnp.concatenate(
            [scores(i, high), high * held_valid[...], low * held_valid[...]], axis=0
        )

    def finish(i, applied):
        values = state(i, 1)
        whole = jnp.concatenate([value_t[head[i]], values, values], axis=1)
        result = dot(whole, applied).T.astype(BF)
        out_own[i] = result[0 : BLOCK // 2]
        out_other[i] = result[BLOCK // 2 :]

    lax.fori_loop(0, ITERS // unroll, iterate, 0)
    staggered(apply_last, finish, count, 2)


def unpack_kernel(info, *rest):
    x, _, _, _ = spot(info)
    parts, (out_ref, stage) = rest[: len(GROUPS)], rest[-2:]
    for shifts, part in zip(GROUPS, parts):
        for i in range(len(shifts) * PER):
            h = (x ^ shifts[i // PER]) * PER + i % PER
            stage[h] = part[i]
    out_ref[...] = jnp.swapaxes(stage[...], 0, 1)


def unpack(info, parts, other, shape, base=()):
    rows = shape[0]

    def place(g, info):
        core = info[0] % 2
        return 0, 1 - core if other else core, 0

    return pl.pallas_call(
        unpack_kernel,
        grid_spec=pltpu.PrefetchScalarGridSpec(
            num_scalar_prefetch=1,
            grid=(1,),
            in_specs=[VMEM] * len(parts) + [pl.BlockSpec(memory_space=pl.ANY)] * len(base),
            out_specs=pl.BlockSpec((rows, 16, HD), place),
            scratch_shapes=[pltpu.VMEM((16, rows, HD), BF)],
        ),
        out_shape=jax.ShapeDtypeStruct(shape, BF),
        input_output_aliases={1 + len(parts): 0} if base else {},
        compiler_params=pltpu.CompilerParams(vmem_limit_bytes=12 << 20),
        name="unpack",
    )(info, *parts, *base)


def body(qkv, lengths, reg):
    rows, _, heads, width = qkv.shape
    half = heads // 2
    index = jnp.arange(2, dtype=jnp.int32)
    info = jnp.where(index == 0, lax.axis_index("head"), lax.axis_index("ctx")).astype(jnp.int32)

    def array(shape, dtype=BF):
        return jax.ShapeDtypeStruct(shape, dtype)

    def swap(a):
        return lax.ppermute(a, "head", [(i, i ^ 1) for i in range(2 * NX)])

    def along_x(a, shift):
        return lax.ppermute(
            a, "head", [(i, 2 * ((i // 2) ^ shift) + i % 2) for i in range(2 * NX)]
        )

    def relay(a):
        ring = [(2 * x, 2 * ((x + 1) % NX)) for x in range(NX)]
        back = [(2 * x + 1, 2 * ((x - 1) % NX) + 1) for x in range(NX)]
        return lax.ppermute(a, "head", ring + back)

    def after(a, *others):
        return lax.optimization_barrier((a, *others))[0]

    flat = qkv.reshape(rows, 3 * heads, width)
    first = pltpu.with_memory_space_constraint(flat, pltpu.HBM)
    key_value, query = (1, 2), (0,)
    far_send = pack(info, first, key_value, 8, True, True)
    far_other = swap(far_send)
    far_own = pack(after(info, far_send), flat, key_value, 8, False, True)
    near_send = pack(after(info, far_own), flat, key_value, 8, True)
    near_other = swap(near_send)

    states = array((PER, 2, width, width))

    def sums(shift, own, other):
        return call(functools.partial(sums_kernel, shift), states)(info, lengths, own, other)

    parts = [None] * NX
    hop = sums(2, after(far_own, near_send), far_other)
    parts[2] = relay(hop)
    third = sums(3, after(far_own, hop), far_other)
    parts[3] = along_x(third, 3)
    near_own = pack(after(info, third), flat, key_value, 8, False)
    second = sums(1, near_own, near_other)
    parts[1] = along_x(second, 1)
    parts[2] = relay(parts[2])
    late = after(info, second)
    q_send = pack(late, flat, query, 16, True)
    q_other = swap(q_send)
    q_own = pack(after(info, q_send), flat, query, 16, False)
    parts[0] = sums(0, after(near_own, second), near_other)
    columns = array((half, width, BLOCK))
    prepared = call(
        prepare_kernel,
        [
            array((half, BLOCK, width)),
            columns,
            columns,
            array(columns.shape, F32),
            array((BLOCK, BLOCK)),
            array((1, BLOCK), F32),
        ],
        limit=24,
    )(info, lengths, far_own, far_other, near_own, near_other, q_own, q_other)
    parts, prepared = lax.optimization_barrier((parts, prepared))
    total = call(totals_kernel, states)(info, lengths, *parts)
    places = lax.axis_size("ctx")
    slices = lax.all_to_all(total.reshape(places, -1, width), "ctx", 0, 0, tiled=True)
    entries = call(entries_kernel, array(slices.shape))(info, lengths, slices)
    entry = lax.all_to_all(entries, "ctx", 0, 0, tiled=True).reshape(states.shape)
    masks = (1, 3, 0, 2)
    made = call(functools.partial(states_kernel, masks), [states] * NX)(
        info, lengths, *parts, entry
    )
    before = dict(zip(masks, made))
    for shift in (1, 3):
        before[shift] = along_x(before[shift], shift)

    mine, theirs = [], []
    for shifts in GROUPS:
        count = len(shifts) * PER
        vectors = pltpu.VMEM((count, width, BLOCK), F32)
        result = array((count, rows, width))
        kept, others = call(
            functools.partial(solve_kernel, shifts),
            [result, result],
            [
                pltpu.VMEM((count, width, BLOCK + width), BF),
                pltpu.VMEM((width, BLOCK), BF),
                vectors,
                vectors,
                vectors,
                vectors,
                pltpu.VMEM((count, 1, BLOCK), F32),
            ],
            flops=10**9 * count,
            limit=28,
        )(info, reg, *prepared, *(before[s] for s in shifts))
        if shifts == (0,):
            before[2] = along_x(after(before[2], kept), 2)
        mine.append(kept)
        theirs.append(others)
    theirs[0] = swap(after(theirs[0], mine[1]))
    theirs[1] = swap(theirs[1])
    theirs[2] = swap(theirs[2])
    shape = (rows, heads, width)
    out = unpack(info, mine, False, shape)
    return unpack(info, theirs, True, shape, (out,))


def solution(mesh):
    in_specs = (P(("ctx", "head"), None, None, None), P(), P())
    out_specs = P(("ctx", "head"), None, None)

    return jax.shard_map(body, mesh=mesh, in_specs=in_specs, out_specs=out_specs, check_vma=False)
```
